128 devices in a mesh: rows: 4 (over y_lo, core), cols: 32 (over y_hi, z, x).
Axes of the slice: x: 4, y: 4 (y_hi: 2, y_lo: 2; y = y_hi * 2 + y_lo), z: 4, core: 2. Of those that a mesh axis runs over, the one named last changes fastest.
Arguments:
- features: bfloat16 [128, 1024, 512], P('rows', 'cols'), may hold values from -8 to 8
- dw_kernel: bfloat16 [13, 13, 512], replicated, may hold values from -0.5 to 0.5
- batchnorm_gain: float32 [512], replicated, may hold values from 0.1 to 1.9
- batchnorm_offset: float32 [512], replicated, may hold values from -3 to 3
- w_in: bfloat16 [512, 2048], replicated, may hold values from -0.25 to 0.25
- b_in: float32 [2048], replicated, may hold values from -3 to 3
- w_out: bfloat16 [2048, 512], replicated, may hold values from -0.125 to 0.125
- b_out: float32 [512], replicated, may hold values from -3 to 3
- layer_scale: float32 [512], replicated, may hold values from 0.25 to 1
- w_down: bfloat16 [2, 2, 512, 1024], replicated, may hold values from -0.125 to 0.125
- b_down: float32 [1024], replicated, may hold values from -3 to 3
- cotangent: bfloat16 [1024, 64, 512], P('cols', 'rows'), may hold values from -6 to 6
Outputs:
- coarse: bfloat16 [1024, 64, 512], P('cols', 'rows')
- grad_input: bfloat16 [128, 1024, 512], P('rows', 'cols')
- grad_kernel: float32 [13, 13, 512], replicated
The draws below stay inside these ranges and needn't reach their ends.
All inputs are finite; a program needn't handle non-finite values.
Results may differ from the reference program's by a relative error of at most 0.0095.
Values may be sent and summed in bfloat16 or wider, within the bound.
A program may use at most 128 MiB of HBM per device.

```python
import math
import jax
import jax.numpy as jnp
from jax import lax

C = 512
FF = 2048
C2 = 1024
K = 13
TW = 32
BAND_H = 128
BAND_W = 1024


def draw_features(key, part):
    noise_key = jax.random.fold_in(key, 11)
    offset_key = jax.random.fold_in(key, 12)
    pairing_key = jax.random.fold_in(key, 13)
    field_key = jax.random.fold_in(key, 15)
    sign_key = jax.random.fold_in(key, 16)
    level_key = jax.random.fold_in(key, 17)
    blocks_wide = BAND_W // TW
    pairing = jax.random.permutation(pairing_key, blocks_wide)
    column_block = jnp.arange(BAND_W, dtype=jnp.int32) // TW
    channel_block = jnp.arange(C, dtype=jnp.int32) * blocks_wide // C
    spike_mask = pairing[column_block][:, None] == channel_block[None, :]
    boost = jnp.where(spike_mask, 2.5, 1.0).astype(jnp.float32)
    coarse_rows = (BAND_H + 3) // 4
    coarse_cols = (BAND_W + 3) // 4
    rim_width = (K - 1) // 2
    row_index = jnp.arange(BAND_H, dtype=jnp.int32)
    col_index = jnp.arange(BAND_W, dtype=jnp.int32)
    row_frame = (row_index < rim_width) | (row_index >= BAND_H - rim_width)
    col_frame = (col_index < rim_width) | (col_index >= BAND_W - rim_width)
    frame_mask = row_frame[:, None] | col_frame[None, :]
    frame_sign = (jax.random.randint(sign_key, (C,), 0, 2) * 2 - 1).astype(jnp.float32)
    single_noise = jnp.clip(jax.random.normal(noise_key, (BAND_H, BAND_W, C), jnp.float32), -3.0, 3.0)
    block_field = jnp.clip(jax.random.normal(field_key, (coarse_rows, coarse_cols, C), jnp.float32), -3.0, 3.0)
    offsets = jnp.clip(0.7 * jax.random.normal(offset_key, (C,), jnp.float32), -2.0, 2.0)
    frame_level = jax.random.uniform(level_key, (C,), jnp.float32, 4.0, 6.0)
    block_full = jnp.repeat(jnp.repeat(block_field, 4, axis=0), 4, axis=1)[:BAND_H, :BAND_W]
    base_noise = 0.6 * single_noise + 0.8 * block_full
    interior = offsets + 0.75 * base_noise * boost
    frame_values = frame_sign * frame_level + 0.3 * single_noise
    values = jnp.where(frame_mask[:, :, None], frame_values, interior)
    return jnp.clip(values, -8.0, 8.0).astype(jnp.bfloat16)


def draw_cotangent(key, part):
    noise_key = jax.random.fold_in(key, 21)
    offset_key = jax.random.fold_in(key, 22)
    shape_full = (C2, BAND_H // 2, BAND_W // 2)
    base_noise = jnp.clip(jax.random.normal(noise_key, shape_full, jnp.float32), -4.0, 4.0)
    offsets = jnp.clip(0.4 * jax.random.normal(offset_key, (C2, 1, 1), jnp.float32), -1.5, 1.5)
    values = offsets + base_noise
    return jnp.clip(values, -6.0, 6.0).astype(jnp.bfloat16)


def scatter_about(rng, shape, spread, limit, held_as=jnp.bfloat16):
    array = jax.random.normal(rng, shape, jnp.float32) * spread
    return jnp.minimum(jnp.maximum(array, -limit), limit).astype(held_as)


def setup_inputs(seed: int = 0) -> dict:
    keys = jax.random.split(jax.random.key(seed), 13)
    features = draw_features(jax.random.fold_in(keys[12], 71), 0)
    dw_kernel = scatter_about(keys[1], (K, K, C), (K * K) ** -0.5, 0.5)
    batchnorm_gain = jnp.clip(1.0 + 0.18 * jax.random.normal(keys[2], (C,), jnp.float32), 0.1, 1.9)
    batchnorm_offset = scatter_about(keys[3], (C,), 0.5, 3.0, jnp.float32)
    w_in = scatter_about(keys[4], (C, FF), C ** -0.5, 0.25)
    b_in = scatter_about(keys[5], (FF,), 0.5, 3.0, jnp.float32)
    w_out = scatter_about(keys[6], (FF, C), FF ** -0.5, 0.125)
    b_out = scatter_about(keys[7], (C,), 0.5, 3.0, jnp.float32)
    layer_scale = jnp.clip(jnp.exp(jax.random.uniform(keys[8], (C,), jnp.float32, math.log(0.25), math.log(1.0))), 0.25, 1.0)
    w_down = scatter_about(keys[9], (2, 2, C, C2), (4 * C) ** -0.5, 0.125)
    b_down = scatter_about(keys[10], (C2,), 0.5, 3.0, jnp.float32)
    cotangent = draw_cotangent(jax.random.fold_in(keys[12], 71), 0)
    return dict(features=features, dw_kernel=dw_kernel, batchnorm_gain=batchnorm_gain, batchnorm_offset=batchnorm_offset, w_in=w_in, b_in=b_in, w_out=w_out, b_out=b_out, layer_scale=layer_scale, w_down=w_down, b_down=b_down, cotangent=cotangent)


def depthwise(padded, kernel):
    return lax.conv_general_dilated(padded[None], kernel[:, :, None, :], (1, 1), 'VALID', dimension_numbers=('NHWC', 'HWIO', 'NHWC'), feature_group_count=padded.shape[-1], preferred_element_type=jnp.float32)[0]

def reference(features, dw_kernel, batchnorm_gain, batchnorm_offset, w_in, b_in, w_out, b_out, layer_scale, w_down, b_down, cotangent):
    radius = (K - 1) // 2
    pads = ((radius, radius), (radius, radius), (0, 0))
    x_padded = jnp.pad(features, pads)
    conv_out = depthwise(x_padded, dw_kernel)
    pixel_total = BAND_H * BAND_W
    mean_val = lax.optimization_barrier(jnp.sum(conv_out, axis=(0, 1))) / pixel_total
    centred_input = conv_out - mean_val
    variance = lax.optimization_barrier(jnp.sum(centred_input * centred_input, axis=(0, 1))) / pixel_total
    inverse_deviation = lax.rsqrt(variance + 1e-05)
    standardized_input = centred_input * inverse_deviation
    normalized_input = (standardized_input * batchnorm_gain + batchnorm_offset).astype(jnp.bfloat16)

    def forward_row(pair):
        norm_row, feat_row = pair
        pre_act = jnp.dot(norm_row, w_in, preferred_element_type=jnp.float32) + b_in
        activated = jax.nn.gelu(pre_act).astype(jnp.bfloat16)
        branch = jnp.dot(activated, w_out, preferred_element_type=jnp.float32) + b_out
        return (feat_row.astype(jnp.float32) + layer_scale * branch).astype(jnp.bfloat16)
    summed = lax.map(forward_row, (normalized_input, features))
    blocks = summed.reshape(BAND_H // 2, 2, BAND_W // 2, 2, C).astype(jnp.float32)
    coarse = jnp.einsum('paqbc,abco->opq', blocks, w_down.astype(jnp.float32)) + b_down[:, None, None]
    coarse = coarse.astype(jnp.bfloat16)
    out_grad = jnp.einsum('opq,abco->paqbc', cotangent.astype(jnp.float32), w_down.astype(jnp.float32))
    out_grad = out_grad.reshape(BAND_H, BAND_W, C).astype(jnp.bfloat16)

    def backward_row(pair):
        grad_row, norm_row = pair
        pre_act = jnp.dot(norm_row, w_in, preferred_element_type=jnp.float32) + b_in
        scaled_grad = (layer_scale * grad_row.astype(jnp.float32)).astype(jnp.bfloat16)
        act_grad = jnp.dot(scaled_grad, w_out.T, preferred_element_type=jnp.float32)
        _, pullback = jax.vjp(jax.nn.gelu, pre_act)
        pre_grad = pullback(act_grad)[0].astype(jnp.bfloat16)
        return jnp.dot(pre_grad, w_in.T, preferred_element_type=jnp.float32)
    normalized_gradient = lax.map(backward_row, (out_grad, normalized_input))
    standardized_gradient = normalized_gradient * batchnorm_gain
    gradient_total = lax.optimization_barrier(jnp.sum(standardized_gradient, axis=(0, 1)))
    gradient_product_sum = lax.optimization_barrier(jnp.sum(standardized_gradient * standardized_input, axis=(0, 1)))
    convolution_gradient = (inverse_deviation * (standardized_gradient - gradient_total / pixel_total - standardized_input * gradient_product_sum / pixel_total)).astype(jnp.bfloat16)
    grad_padded = jnp.pad(convolution_gradient, pads)
    back_conv = depthwise(grad_padded, dw_kernel[::-1, ::-1])
    grad_input = (out_grad.astype(jnp.float32) + back_conv).astype(jnp.bfloat16)
    grad_kernel = depthwise(x_padded, convolution_gradient) * lax.rsqrt(jnp.float32(pixel_total))
    return (coarse, grad_input, grad_kernel)
```

```python
import functools

import jax
import jax.numpy as jnp
import numpy as np
from jax import lax
from jax.experimental import pallas as pl
from jax.experimental.pallas import tpu as pltpu
from jax.sharding import PartitionSpec as P

MESH = pl.DeviceIdType.MESH


@functools.lru_cache(maxsize=None)
def dft_tables(tile_h, tile_w, radius):
    nh, nw = tile_h + 2 * radius, tile_w + 2 * radius
    freqs = []
    for u in range(nh):
        for v in range(nw // 2 + 1):
            if v in (0, nw // 2) and u > nh // 2:
                continue
            own = v in (0, nw // 2) and u in (0, nh // 2)
            freqs.append((u, v, 1.0 if own else 2.0))
    count = -(-len(freqs) // 16) * 16
    u = np.zeros(count)
    v = np.zeros(count)
    weight = np.zeros(count)
    for index, (a, b, w) in enumerate(freqs):
        u[index], v[index], weight[index] = a, b, w / (nh * nw)

    def rows(points):
        p = np.asarray(points)
        turns = (np.outer(u, p[:, 0]) % nh) / nh + (np.outer(v, p[:, 1]) % nw) / nw
        live = (weight > 0)[:, None]
        angle = 2.0 * np.pi * turns
        table = np.concatenate([np.cos(angle) * live, -np.sin(angle) * live], axis=0)
        table[np.abs(table) < 1e-9] = 0.0
        return table.astype(jnp.bfloat16)

    inner = [(h, w) for h in range(tile_h) for w in range(tile_w)]
    top = [(h - radius, w) for h in range(radius) for w in range(tile_w)]
    bottom = [(tile_h + h, w) for h in range(radius) for w in range(tile_w)]
    side = [(h - radius, w) for w in range(radius) for h in range(nh)]
    left = [(h, w - radius) for h, w in side]
    right = [(h, w + tile_w) for h, w in side]
    taps = [(i - radius, j - radius) for i in range(2 * radius + 1) for j in range(2 * radius + 1)]
    inner_t, rim_t, tap_t = rows(inner), rows(top + bottom + left + right), rows(taps)
    total = inner_t.astype(np.float64).sum(1) + rim_t.astype(np.float64).sum(1)
    leak = total / (nh * nw)
    leak[0] = 0.0
    return inner_t, rim_t, tap_t, weight.astype(np.float32), leak.astype(np.float32)


def rim_pixels(block, radius):
    rows, cols = lax.axis_size("rows"), lax.axis_size("cols")
    down = [(i, i + 1) for i in range(rows - 1)]
    up = [(b, a) for a, b in down]
    east = [(i, i + 1) for i in range(cols - 1)]
    west = [(b, a) for a, b in east]
    top = lax.ppermute(block[-radius:], "rows", down)
    bottom = lax.ppermute(block[:radius], "rows", up)
    channel_count = block.shape[-1]

    def strip(sel):
        tall = jnp.concatenate([top[:, sel], block[:, sel], bottom[:, sel]], axis=0)
        return jnp.transpose(tall, (1, 0, 2))

    left = lax.ppermute(strip(slice(-radius, None)), "cols", east)
    right = lax.ppermute(strip(slice(0, radius)), "cols", west)
    return jnp.concatenate(
        [p.reshape(-1, channel_count) for p in (top, bottom, left, right)], axis=0
    )


def fdot(a, b):
    return jnp.dot(a, b, preferred_element_type=jnp.float32)


def tdot(a, b):
    return lax.dot_general(a, b, (((0,), (0,)), ((), ())), preferred_element_type=jnp.float32)


NEAR_X = 4


def group_ids(rows, cols):
    r, c = lax.axis_index("rows"), lax.axis_index("cols")
    x, far = c % NEAR_X, c // NEAR_X
    fars = cols // NEAR_X
    near = r * NEAR_X + x
    return r, x, far, fars, near, rows * NEAR_X


def near_dev(index, far):
    return {"rows": index // NEAR_X, "cols": far * NEAR_X + index % NEAR_X}


def far_dev(r, x, index):
    return {"rows": r, "cols": index * NEAR_X + x}


def greet(near, nears, far, fars, r, x):
    barrier = pltpu.get_barrier_semaphore()
    for k in range(1, nears):
        pl.semaphore_signal(
            barrier, inc=1, device_id=near_dev((near + k) % nears, far), device_id_type=MESH
        )
    for k in range(1, fars):
        pl.semaphore_signal(
            barrier, inc=1, device_id=far_dev(r, x, (far + k) % fars), device_id_type=MESH
        )
    pl.semaphore_wait(barrier, nears + fars - 2)


def take(ref, count, sem):
    piece = ref.at[pl.ds(0, count)]
    pltpu.make_async_copy(piece, piece, sem).wait()


def moments_kernel(mode, points, rows, cols, in_ref, out_ref, near_buf, far_buf, mid, sems):
    r, x, far, fars, near, nears = group_ids(rows, cols)
    greet(near, nears, far, fars, r, x)
    for k in range(1, nears):
        pltpu.make_async_remote_copy(
            in_ref, near_buf.at[near], sems.at[0], sems.at[1],
            device_id=near_dev((near + k) % nears, far), device_id_type=MESH,
        ).start()
    near_buf[near] = in_ref[...]
    take(near_buf, nears - 1, sems.at[1])
    take(near_buf, nears - 1, sems.at[0])

    def merge(buf, count, each):
        if mode == "sum":
            return jnp.sum(buf[...], axis=0)
        half = buf.shape[1] // 2
        means = buf[:, :half]
        mean = jnp.sum(means, axis=0) * (1.0 / count)
        gap = means - mean[None]
        spread = jnp.sum(buf[:, half:], axis=0) + each * jnp.sum(gap * gap, axis=0)
        return jnp.concatenate([mean, spread], axis=0)

    mid[...] = merge(near_buf, nears, float(points))
    for k in range(1, fars):
        pltpu.make_async_remote_copy(
            mid, far_buf.at[far], sems.at[2], sems.at[3],
            device_id=far_dev(r, x, (far + k) % fars), device_id_type=MESH,
        ).start()
    far_buf[far] = mid[...]
    take(far_buf, fars - 1, sems.at[3])
    take(far_buf, fars - 1, sems.at[2])
    out_ref[...] = merge(far_buf, fars, float(points * nears))


def exchange_moments(first, second, mode, points, collective_id):
    rows, cols = lax.axis_size("rows"), lax.axis_size("cols")
    width = first.shape[0]
    lines = width // 128
    packed = jnp.concatenate([first.reshape(lines, 128), second.reshape(lines, 128)], axis=0)
    merged = pl.pallas_call(
        functools.partial(moments_kernel, mode, points, rows, cols),
        out_shape=jax.ShapeDtypeStruct(packed.shape, jnp.float32),
        in_specs=[pl.BlockSpec(memory_space=pltpu.VMEM)],
        out_specs=pl.BlockSpec(memory_space=pltpu.VMEM),
        scratch_shapes=[
            pltpu.VMEM((rows * NEAR_X,) + packed.shape, jnp.float32),
            pltpu.VMEM((cols // NEAR_X,) + packed.shape, jnp.float32),
            pltpu.VMEM(packed.shape, jnp.float32),
            pltpu.SemaphoreType.DMA((4,)),
        ],
        compiler_params=pltpu.CompilerParams(collective_id=collective_id, has_side_effects=True),
        name="moments_" + mode,
    )(packed)
    return merged[:lines].reshape(width), merged[lines:].reshape(width)


def total_kernel(rows, cols, in_ref, out_ref, near_buf, far_buf, share, piece, sems):
    r, x, far, fars, near, nears = group_ids(rows, cols)
    greet(near, nears, far, fars, r, x)
    for k in range(1, nears):
        peer = (near + k) % nears
        pltpu.make_async_remote_copy(
            in_ref.at[peer], near_buf.at[near], sems.at[0], sems.at[1],
            device_id=near_dev(peer, far), device_id_type=MESH,
        ).start()
    near_buf[near] = in_ref[near]
    take(near_buf, nears - 1, sems.at[1])
    share[...] = jnp.sum(near_buf[...], axis=0)
    for k in range(1, fars):
        peer = (far + k) % fars
        pltpu.make_async_remote_copy(
            share.at[peer], far_buf.at[far], sems.at[2], sems.at[3],
            device_id=far_dev(r, x, peer), device_id_type=MESH,
        ).start()
    far_buf[far] = share[far]
    take(far_buf, fars - 1, sems.at[3])
    piece[...] = jnp.sum(far_buf[...], axis=0)
    for k in range(1, fars):
        pltpu.make_async_remote_copy(
            piece, out_ref.at[near, far], sems.at[4], sems.at[5],
            device_id=far_dev(r, x, (far + k) % fars), device_id_type=MESH,
        ).start()
    out_ref[near, far] = piece[...]
    take(far_buf, fars - 1, sems.at[5])
    for k in range(1, nears):
        pltpu.make_async_remote_copy(
            out_ref.at[near], out_ref.at[near], sems.at[6], sems.at[7],
            device_id=near_dev((near + k) % nears, far), device_id_type=MESH,
        ).start()
    take(near_buf, nears - 1, sems.at[7])
    take(near_buf, nears - 1, sems.at[0])
    take(far_buf, fars - 1, sems.at[2])
    take(far_buf, fars - 1, sems.at[4])
    take(near_buf, nears - 1, sems.at[6])


def sum_everywhere(value, collective_id):
    rows, cols = lax.axis_size("rows"), lax.axis_size("cols")
    nears, fars = rows * NEAR_X, cols // NEAR_X
    taps, width = value.shape
    lines = -(-(taps * width) // (nears * fars * 128))
    flat = jnp.pad(value.reshape(-1, 128), ((0, nears * fars * lines - taps * width // 128), (0, 0)))
    parts = flat.reshape(nears, fars, lines, 128)
    total = pl.pallas_call(
        functools.partial(total_kernel, rows, cols),
        out_shape=jax.ShapeDtypeStruct(parts.shape, jnp.float32),
        in_specs=[pl.BlockSpec(memory_space=pltpu.VMEM)],
        out_specs=pl.BlockSpec(memory_space=pltpu.VMEM),
        scratch_shapes=[
            pltpu.VMEM((nears, fars, lines, 128), jnp.float32),
            pltpu.VMEM((fars, lines, 128), jnp.float32),
            pltpu.VMEM((fars, lines, 128), jnp.float32),
            pltpu.VMEM((lines, 128), jnp.float32),
            pltpu.SemaphoreType.DMA((8,)),
        ],
        compiler_params=pltpu.CompilerParams(collective_id=collective_id, has_side_effects=True),
        name="kernel_total",
    )(parts)
    return total.reshape(-1, 128)[: taps * width // 128].reshape(taps, width)


def per_device(
    features,
    dw_kernel,
    batchnorm_gain,
    batchnorm_offset,
    w_in,
    b_in,
    w_out,
    b_out,
    layer_scale,
    w_down,
    b_down,
    cotangent,
):
    tile_height, tile_width, channel_count = features.shape
    radius = (dw_kernel.shape[0] - 1) // 2
    pixel_total = tile_height * lax.axis_size("rows") * tile_width * lax.axis_size("cols")
    pixels = tile_height * tile_width
    inner_t, rim_t, tap_t, weight, leak = dft_tables(tile_height, tile_width, radius)
    half = weight.shape[0]
    weight, leak = jnp.asarray(weight)[:, None], jnp.asarray(leak)[:, None]

    def spectrum(inner, rim):
        spec = inner + fdot(rim_t, rim)
        spec = spec - leak * spec[:1]
        return spec[:half], spec[half:]

    def pixels_of(real, imag, table):
        spec = jnp.concatenate([real * weight, imag * weight], axis=0).astype(jnp.bfloat16)
        return tdot(table, spec)

    tap_spec = fdot(tap_t, dw_kernel.reshape(-1, channel_count))
    tap_re, tap_im = tap_spec[:half], tap_spec[half:]
    feat_inner = fdot(inner_t, features.reshape(pixels, channel_count))
    feat_re, feat_im = spectrum(feat_inner, rim_pixels(features, radius))
    conv_out = pixels_of(
        feat_re * tap_re + feat_im * tap_im, feat_im * tap_re - feat_re * tap_im, inner_t
    )
    local_mean = jnp.sum(conv_out, axis=0) / pixels
    local_gap = conv_out - local_mean
    mean_val, spread = exchange_moments(
        local_mean, jnp.sum(local_gap * local_gap, axis=0), "merge", pixels, 1
    )
    variance = spread / pixel_total
    inverse_deviation = lax.rsqrt(variance + 1e-05)
    standardized_input = (conv_out - mean_val) * inverse_deviation
    normalized_input = (
        (standardized_input * batchnorm_gain + batchnorm_offset)
        .astype(jnp.bfloat16)
    )
    pre_act = jnp.dot(normalized_input, w_in, preferred_element_type=jnp.float32) + b_in
    activated = jax.nn.gelu(pre_act).astype(jnp.bfloat16)
    branch = jnp.dot(activated, w_out, preferred_element_type=jnp.float32) + b_out
    flat_feat = features.reshape(tile_height * tile_width, channel_count).astype(jnp.float32)
    summed = (flat_feat + layer_scale * branch).astype(jnp.bfloat16)
    blocks = summed.reshape(tile_height // 2, 2, tile_width // 2, 2, channel_count)
    local_coarse = (
        jnp.einsum("paqbc,abco->opq", blocks, w_down, preferred_element_type=jnp.float32)
        + b_down[:, None, None]
    )
    coarse = lax.all_to_all(
        local_coarse.astype(jnp.bfloat16), "cols", split_axis=0, concat_axis=2, tiled=True
    )
    tile_cot = lax.all_to_all(cotangent, "cols", split_axis=2, concat_axis=0, tiled=True)
    out_grad = jnp.einsum("opq,abco->paqbc", tile_cot, w_down, preferred_element_type=jnp.float32)
    out_grad = out_grad.reshape(tile_height * tile_width, channel_count).astype(jnp.bfloat16)
    scaled_grad = (layer_scale * out_grad.astype(jnp.float32)).astype(jnp.bfloat16)
    act_grad = jnp.dot(scaled_grad, w_out.T, preferred_element_type=jnp.float32)
    _, pullback = jax.vjp(jax.nn.gelu, pre_act)
    pre_grad = pullback(act_grad)[0].astype(jnp.bfloat16)
    normalized_gradient = jnp.dot(pre_grad, w_in.T, preferred_element_type=jnp.float32)
    standardized_gradient = normalized_gradient * batchnorm_gain
    gradient_total, gradient_product_sum = exchange_moments(
        jnp.sum(standardized_gradient, axis=0),
        jnp.sum(standardized_gradient * standardized_input, axis=0),
        "sum", pixels, 2,
    )
    convolution_gradient = (
        inverse_deviation
        * (
            standardized_gradient
            - gradient_total / pixel_total
            - standardized_input * (gradient_product_sum / pixel_total)
        )
    ).astype(jnp.bfloat16)
    grad_inner = fdot(inner_t, convolution_gradient)
    own_re, own_im = grad_inner[:half], grad_inner[half:]
    kernel_term = pixels_of(
        feat_re * own_re + feat_im * own_im, feat_im * own_re - feat_re * own_im, tap_t
    )
    grad_kernel = sum_everywhere(kernel_term, 3) * lax.rsqrt(jnp.float32(pixel_total))
    grad_kernel = grad_kernel.reshape(dw_kernel.shape)
    rim = rim_pixels(
        convolution_gradient.reshape(tile_height, tile_width, channel_count), radius
    )
    grad_re, grad_im = spectrum(grad_inner, rim)
    back_conv = pixels_of(
        grad_re * tap_re - grad_im * tap_im, grad_re * tap_im + grad_im * tap_re, inner_t
    )
    grad_input = (
        (out_grad.astype(jnp.float32) + back_conv)
        .astype(jnp.bfloat16)
        .reshape(tile_height, tile_width, channel_count)
    )
    return (coarse, grad_input, grad_kernel)


def solution(mesh):
    in_specs = (
        P("rows", "cols", None),
        P(),
        P(),
        P(),
        P(),
        P(),
        P(),
        P(),
        P(),
        P(),
        P(),
        P("cols", "rows", None),
    )
    out_specs = (P("cols", "rows", None), P("rows", "cols", None), P())
    return jax.shard_map(
        per_device, mesh=mesh, in_specs=in_specs, out_specs=out_specs, check_vma=False
    )
```

```python
import functools

import jax
import jax.numpy as jnp
import numpy as np
from jax import lax
from jax.experimental import pallas as pl
from jax.experimental.pallas import tpu as pltpu
from jax.sharding import PartitionSpec as P

MESH = pl.DeviceIdType.MESH
F32 = jnp.float32
BF16 = jnp.bfloat16
NEAR_X = 4
GROUP = 8
HALF = 1024
CHUNK = 256


def balanced(table):
    low = table.astype(jnp.bfloat16)
    bits = low.view(np.uint16)
    up = (bits + 1).astype(np.uint16).view(jnp.bfloat16).astype(np.float64)
    down = (bits - 1).astype(np.uint16).view(jnp.bfloat16).astype(np.float64)
    value = low.astype(np.float64)
    out = value.copy()
    for row in range(table.shape[0]):
        excess = (value[row] - table[row]).sum()
        if excess == 0.0:
            continue
        live = np.nonzero(np.abs(table[row]) > 0.004)[0]
        steps = np.stack([up[row, live], down[row, live]]) - value[row, live]
        order = np.argsort(-np.abs(steps[0]), kind="stable")
        for spot in order:
            for step in steps[:, spot]:
                if abs(excess + step) < abs(excess) - 0.25 * abs(step):
                    out[row, live[spot]] += step
                    excess += step
                    break
    return out.astype(jnp.bfloat16)


@functools.lru_cache(maxsize=None)
def dft_tables(tile_h, tile_w, radius):
    nh, nw = tile_h + 2 * radius, tile_w + 2 * radius
    u, v, weight = np.zeros(HALF), np.zeros(HALF), np.zeros(HALF)
    index = 0
    for a in range(nh):
        for b in range(nw // 2 + 1):
            edge = b in (0, nw // 2)
            if edge and a > nh // 2:
                continue
            u[index], v[index] = a, b
            weight[index] = 1.0 if edge and a in (0, nh // 2) else 2.0
            index += 1
    live = weight > 0

    def rows(points):
        p = np.asarray(points)
        turns = (np.outer(u, p[:, 0]) % nh) / nh + (np.outer(v, p[:, 1]) % nw) / nw
        angle = 2.0 * np.pi * turns
        table = np.concatenate([np.cos(angle) * live[:, None], -np.sin(angle) * live[:, None]])
        table[np.abs(table) < 1e-9] = 0.0
        return table

    inner = [(h, w) for h in range(tile_h) for w in range(tile_w)]
    wests = range(-GROUP, 0)
    easts = range(tile_w, tile_w + GROUP)
    norths = range(-radius, 0)
    souths = range(tile_h, tile_h + radius)
    rim = [(h, w) for hs in (norths, souths) for h in hs for w in range(tile_w)]
    rim += [(h, w) for ws in (wests, easts) for h in range(tile_h) for w in ws]
    rim += [(h, w) for hs in (norths, souths) for ws in (wests, easts) for h in hs for w in ws]
    kept = np.asarray([-radius <= w < tile_w + radius for _, w in rim])
    taps = [(i, j) for i in range(-radius, radius + 1) for j in range(-radius, radius + 1)]
    both = balanced(np.concatenate([rows(inner), rows(rim) * kept[None]], axis=1))
    count = len(inner)
    tap_t = rows(taps)
    doubled = np.concatenate([weight, weight])[None]
    f_tap = np.pad(tap_t, ((0, 0), (0, CHUNK - len(taps)))).astype(jnp.bfloat16)
    f_out = (rows(inner).T * doubled).astype(jnp.bfloat16)
    tap_lines = -(-len(taps) // 48) * 48
    g_tap = np.pad(tap_t.T * doubled, ((0, tap_lines - len(taps)), (0, 0))).astype(jnp.bfloat16)
    return both[:, :count], both[:, count:], f_tap, f_out, g_tap


@functools.lru_cache(maxsize=None)
def phase_table(tile_w):
    table = np.zeros((CHUNK, CHUNK), np.float32)
    lines = CHUNK // tile_w
    for h in range(lines):
        for w in range(tile_w):
            plane = (h % 2) * 2 + w % 2
            table[plane * 64 + (h // 2) * (tile_w // 2) + w // 2, h * tile_w + w] = 1.0
    return table.astype(jnp.bfloat16)


def fdot(a, b):
    return jnp.dot(a, b, preferred_element_type=F32)


def ndot(a, b):
    return lax.dot_general(a, b, (((1,), (1,)), ((), ())), preferred_element_type=F32)


def rows_of(step, size=CHUNK):
    return pl.ds(pl.multiple_of(step * size, size), size)


def swap_blocks(parts):
    lane = lax.broadcasted_iota(jnp.int32, parts[0].shape, 1) // 16
    parts = list(parts)
    for k in (1, 2, 4):
        low = (lane // k) % 2 == 0
        for i in range(8):
            if i & k:
                continue
            a, b = parts[i], parts[i | k]
            parts[i] = jnp.where(low, a, pltpu.roll(b, 16 * k, 1))
            parts[i | k] = jnp.where(low, pltpu.roll(a, 128 - 16 * k, 1), b)
    return parts


class Place:
    def __init__(self, rows, cols):
        self.rows, self.cols = rows, cols
        self.r, self.c = lax.axis_index("rows"), lax.axis_index("cols")
        self.x, self.far = self.c % NEAR_X, self.c // NEAR_X
        self.fars, self.nears = cols // NEAR_X, rows * NEAR_X
        self.near = self.r * NEAR_X + self.x

    def near_dev(self, k):
        peer = (self.near + k) % self.nears
        return peer, {"rows": peer // NEAR_X, "cols": self.far * NEAR_X + peer % NEAR_X}

    def far_dev(self, k):
        peer = (self.far + k) % self.fars
        return peer, {"rows": self.r, "cols": peer * NEAR_X + self.x}

    def col_dev(self, k):
        peer = (self.c + k) % self.cols
        return peer, {"rows": self.r, "cols": peer}

    def inside(self, dr, dc):
        r, c = self.r + dr, self.c + dc
        return (r >= 0) & (r < self.rows) & (c >= 0) & (c < self.cols)

    def rim_dev(self, dr, dc):
        return {"rows": self.r + dr, "cols": self.c + dc}

    def greet(self):
        barrier = pltpu.get_barrier_semaphore()
        for dr, dc in STEPS:
            @pl.when(self.inside(dr, dc))
            def _():
                pl.semaphore_signal(
                    barrier, inc=1, device_id=self.rim_dev(dr, dc), device_id_type=MESH
                )
        for count, dev in (
            (self.nears, self.near_dev), (self.fars, self.far_dev), (self.cols, self.col_dev)
        ):
            for k in range(1, count):
                pl.semaphore_signal(barrier, inc=1, device_id=dev(k)[1], device_id_type=MESH)

    def met(self):
        def beside(at, size):
            return 1 + (at + size - 1) // size + (2 * size - 2 - at) // size

        around = beside(self.r, self.rows) * beside(self.c, self.cols) - 1
        pl.semaphore_wait(
            pltpu.get_barrier_semaphore(), around + self.nears + self.fars + self.cols - 3
        )


STEPS = ((1, 0), (-1, 0), (0, 1), (0, -1), (1, 1), (1, -1), (-1, 1), (-1, -1))


def send(src, dst, sems, slot, dev):
    pltpu.make_async_remote_copy(
        src, dst, sems.at[slot], sems.at[slot + 1], device_id=dev, device_id_type=MESH
    ).start()


def take(ref, sem):
    pltpu.make_async_copy(ref, ref, sem).wait()


def rim_pieces(block, radius, tb, lr, corner):
    lines, groups = block.shape[0], block.shape[1]
    south, north = pl.ds(lines - radius, radius), pl.ds(0, radius)
    last = groups - 1
    return (
        (block.at[south], tb.at[0]),
        (block.at[north], tb.at[1]),
        (block.at[:, last], lr.at[0]),
        (block.at[:, 0], lr.at[1]),
        (block.at[south, last], corner.at[0]),
        (block.at[south, 0], corner.at[1]),
        (block.at[north, last], corner.at[2]),
        (block.at[north, 0], corner.at[3]),
    )


def start_rim(place, pieces, sems):
    for (dr, dc), (src, dst), k in zip(STEPS, pieces, range(8)):
        @pl.when(place.inside(dr, dc))
        def _():
            send(src, dst, sems, 2 * k, place.rim_dev(dr, dc))


def finish_rim(place, pieces, sems, tb, lr, corner, rim):
    for (dr, dc), (_, dst), k in zip(STEPS, pieces, range(8)):
        @pl.when(place.inside(-dr, -dc))
        def _():
            take(dst, sems.at[2 * k + 1])

        @pl.when(jnp.logical_not(place.inside(-dr, -dc)))
        def _():
            dst[...] = jnp.zeros(dst.shape, BF16)

    channels = rim.shape[1]
    at = 0
    for ref in (tb, lr, corner):
        count = int(np.prod(ref.shape[:-1]))
        flat = ref[...].astype(F32).reshape(count, channels).astype(BF16)
        rim[at : at + count] = flat
        at += count


def drain_rim(place, pieces, sems):
    for (dr, dc), (_, dst), k in zip(STEPS, pieces, range(8)):
        @pl.when(place.inside(dr, dc))
        def _():
            take(dst, sems.at[2 * k])


def lines_of(row):
    return jnp.concatenate([row[:, k * 128 : (k + 1) * 128] for k in range(row.shape[1] // 128)], 0)


def row_of(lines):
    return jnp.concatenate([lines[k : k + 1] for k in range(lines.shape[0])], 1)


def merge_moments(buf, count, each):
    half = buf.shape[1] // 2
    means = buf[:, :half]
    mean = jnp.sum(means, axis=0) * (1.0 / count)
    gap = means - mean[None]
    spread = jnp.sum(buf[:, half:], axis=0) + each * jnp.sum(gap * gap, axis=0)
    return jnp.concatenate([mean, spread], axis=0)


def forward_kernel(
    rows, cols, radius,
    feat_hbm, feat4_hbm, cot_hbm, tap_hbm, fin_hbm, frim_hbm, ftap_hbm, fout_hbm, down_hbm, phase_hbm,
    conv_ref, spec_ref, moments_ref, grad_ref,
    feat, cot, taps, fin, frim, ftap, fout, down, phase,
    cot32, spread, cot_in, tap_spec, mixed, tb, lr, corner, rim, planes,
    near_buf, far_buf, mine, mid, in_sems, rim_sems, sems,
):
    place = Place(rows, cols)
    loads = [
        pltpu.make_async_copy(src, dst, in_sems.at[k])
        for k, (src, dst) in enumerate((
            (cot_hbm, cot), (tap_hbm, taps), (ftap_hbm, ftap), (feat_hbm, feat), (fin_hbm, fin),
            (frim_hbm, frim), (fout_hbm, fout), (down_hbm, down), (phase_hbm, phase),
        ))
    ]
    for load in loads:
        load.start()
    place.greet()

    loads[0].wait()
    outs, lines, width = cot.shape
    for tg in range(width // 128):
        cot32[tg] = cot[:, :, tg * 128 : (tg + 1) * 128].astype(F32).reshape(outs * lines, 128)
        for pg in range(lines // 8):
            parts = swap_blocks([
                cot32[tg, pl.ds(pg * 8 + k, outs, stride=lines), :] for k in range(8)
            ])
            for k in range(8):
                spread[tg * 8 + k, :, pg * 128 : (pg + 1) * 128] = parts[k].astype(BF16)
    place.met()
    pieces = rim_pieces(feat4_hbm, radius, tb, lr, corner)
    start_rim(place, pieces, rim_sems)
    for k in range(1, cols):
        peer, dev = place.col_dev(k)
        send(spread.at[peer], cot_in.at[place.c], sems, 0, dev)
    cot_in[place.c] = spread[place.c]

    loads[1].wait()
    loads[2].wait()

    @pl.loop(0, 2 * HALF // CHUNK)
    def _(m):
        tap_spec[rows_of(m)] = fdot(ftap[rows_of(m)], taps[...])

    loads[3].wait()
    loads[4].wait()

    @pl.loop(0, 2 * HALF // CHUNK)
    def _(m):
        spec_ref[rows_of(m)] = fdot(fin[rows_of(m)], feat[...])

    finish_rim(place, pieces, rim_sems, tb, lr, corner, rim)
    loads[5].wait()

    @pl.loop(0, HALF // CHUNK)
    def _(m):
        re, im = rows_of(m), rows_of(m + HALF // CHUNK)
        fr = spec_ref[re] + fdot(frim[re], rim[...])
        fi = spec_ref[im] + fdot(frim[im], rim[...])
        spec_ref[re], spec_ref[im] = fr, fi
        kr, ki = tap_spec[re], tap_spec[im]
        mixed[re] = (fr * kr + fi * ki).astype(BF16)
        mixed[im] = (fi * kr - fr * ki).astype(BF16)

    loads[6].wait()
    pixels = conv_ref.shape[0]
    channels = conv_ref.shape[1]
    area = (lines * 2 + 2 * radius) * (pixels // (lines * 2) + 2 * radius)

    def invert(m, total):
        block = fdot(fout[rows_of(m)], mixed[...]) * (1.0 / area)
        conv_ref[rows_of(m)] = block
        return total + jnp.sum(block, axis=0, keepdims=True)

    zero = jnp.zeros((1, channels), F32)
    mean = lax.fori_loop(0, pixels // CHUNK, invert, zero) * (1.0 / pixels)

    def scatter(m, total):
        gap = conv_ref[rows_of(m)] - mean
        return total + jnp.sum(gap * gap, axis=0, keepdims=True)

    around = lax.fori_loop(0, pixels // CHUNK, scatter, zero)
    mine[...] = jnp.concatenate([lines_of(mean), lines_of(around)], axis=0)
    for k in range(1, place.nears):
        send(mine, near_buf.at[place.near], sems, 2, place.near_dev(k)[1])
    near_buf[place.near] = mine[...]

    take(cot_in.at[pl.ds(0, cols - 1)], sems.at[1])
    loads[7].wait()
    loads[8].wait()
    tall = cot_in[...].reshape(cols * outs, lines * lines).astype(F32).T.astype(BF16)
    for ab in range(4):
        plane = ndot(tall, down[ab]).astype(BF16)
        for k in range(pixels // CHUNK):
            planes[k, ab * 64 : (ab + 1) * 64] = plane[k * 64 : (k + 1) * 64]
    take(near_buf.at[pl.ds(0, place.nears - 1)], sems.at[3])
    mid[...] = merge_moments(near_buf, place.nears, float(pixels))
    for k in range(1, place.fars):
        send(mid, far_buf.at[place.far], sems, 4, place.far_dev(k)[1])
    far_buf[place.far] = mid[...]
    for k in range(pixels // CHUNK):
        grad_ref[k * CHUNK : (k + 1) * CHUNK] = lax.dot_general(
            phase[...], planes[k], (((0,), (0,)), ((), ())), preferred_element_type=F32
        ).astype(BF16)
    take(far_buf.at[pl.ds(0, place.fars - 1)], sems.at[5])
    moments_ref[...] = merge_moments(far_buf, place.fars, float(pixels * place.nears))
    drain_rim(place, pieces, rim_sems)
    take(cot_in.at[pl.ds(0, cols - 1)], sems.at[0])
    take(near_buf.at[pl.ds(0, place.nears - 1)], sems.at[2])
    take(far_buf.at[pl.ds(0, place.fars - 1)], sems.at[4])


def forward_part(features, cotangent, dw_kernel, w_down):
    rows, cols = lax.axis_size("rows"), lax.axis_size("cols")
    tile_h, tile_w, channels = features.shape
    radius = (dw_kernel.shape[0] - 1) // 2
    pixels = tile_h * tile_w
    fin, frim, ftap, fout, _ = dft_tables(tile_h, tile_w, radius)
    groups = tile_w // GROUP
    taps = dw_kernel.reshape(-1, channels)
    taps = jnp.pad(taps, ((0, CHUNK - taps.shape[0]), (0, 0)))
    outs, lines, width = cotangent.shape
    operands = (
        features.reshape(pixels, channels),
        features.reshape(tile_h, groups, GROUP, channels),
        cotangent,
        taps,
        jnp.asarray(fin), jnp.asarray(frim), jnp.asarray(ftap), jnp.asarray(fout),
        w_down.reshape(4, channels, w_down.shape[-1]),
        jnp.asarray(phase_table(tile_w)),
    )
    stats_shape = (2 * channels // 128, 128)
    vm = pltpu.VMEM
    scratch = [vm(operands[k].shape, BF16) for k in (0, 2, 3, 4, 5, 6, 7, 8, 9)]
    scratch += [
        vm((width // 128, outs * lines, 128), F32),
        vm((cols, outs, lines * lines), BF16),
        vm((cols, outs, lines * lines), BF16),
        vm((2 * HALF, channels), F32),
        vm((2 * HALF, channels), BF16),
        vm((2, radius, groups, GROUP, channels), BF16),
        vm((2, tile_h, GROUP, channels), BF16),
        vm((4, radius, GROUP, channels), BF16),
        vm((frim.shape[1], channels), BF16),
        vm((pixels // CHUNK, CHUNK, channels), BF16),
        vm((rows * NEAR_X,) + stats_shape, F32),
        vm((cols // NEAR_X,) + stats_shape, F32),
        vm(stats_shape, F32),
        vm(stats_shape, F32),
        pltpu.SemaphoreType.DMA((9,)),
        pltpu.SemaphoreType.DMA((16,)),
        pltpu.SemaphoreType.DMA((6,)),
    ]
    return pl.pallas_call(
        functools.partial(forward_kernel, rows, cols, radius),
        out_shape=(
            jax.ShapeDtypeStruct((pixels, channels), F32),
            jax.ShapeDtypeStruct((2 * HALF, channels), F32),
            jax.ShapeDtypeStruct(stats_shape, F32),
            jax.ShapeDtypeStruct((pixels, channels), BF16),
        ),
        in_specs=[pl.BlockSpec(memory_space=pl.ANY)] * len(operands),
        out_specs=[pl.BlockSpec(memory_space=pltpu.VMEM)] * 4,
        scratch_shapes=scratch,
        compiler_params=pltpu.CompilerParams(
            collective_id=1, has_side_effects=True, vmem_limit_bytes=60 << 20
        ),
        name="forward_part",
    )(*operands)


def group_ids(rows, cols):
    r, c = lax.axis_index("rows"), lax.axis_index("cols")
    x, far = c % NEAR_X, c // NEAR_X
    fars = cols // NEAR_X
    near = r * NEAR_X + x
    return r, x, far, fars, near, rows * NEAR_X


def near_dev(index, far):
    return {"rows": index // NEAR_X, "cols": far * NEAR_X + index % NEAR_X}


def far_dev(r, x, index):
    return {"rows": r, "cols": index * NEAR_X + x}


def greet(near, nears, far, fars, r, x):
    barrier = pltpu.get_barrier_semaphore()
    for k in range(1, nears):
        pl.semaphore_signal(
            barrier, inc=1, device_id=near_dev((near + k) % nears, far), device_id_type=MESH
        )
    for k in range(1, fars):
        pl.semaphore_signal(
            barrier, inc=1, device_id=far_dev(r, x, (far + k) % fars), device_id_type=MESH
        )
    pl.semaphore_wait(barrier, nears + fars - 2)


def take_some(ref, count, sem):
    piece = ref.at[pl.ds(0, count)]
    pltpu.make_async_copy(piece, piece, sem).wait()


def moments_kernel(mode, points, rows, cols, in_ref, out_ref, near_buf, far_buf, mid, sems):
    r, x, far, fars, near, nears = group_ids(rows, cols)
    greet(near, nears, far, fars, r, x)
    for k in range(1, nears):
        pltpu.make_async_remote_copy(
            in_ref, near_buf.at[near], sems.at[0], sems.at[1],
            device_id=near_dev((near + k) % nears, far), device_id_type=MESH,
        ).start()
    near_buf[near] = in_ref[...]
    take_some(near_buf, nears - 1, sems.at[1])
    take_some(near_buf, nears - 1, sems.at[0])

    def merge(buf, count, each):
        if mode == "sum":
            return jnp.sum(buf[...], axis=0)
        half = buf.shape[1] // 2
        means = buf[:, :half]
        mean = jnp.sum(means, axis=0) * (1.0 / count)
        gap = means - mean[None]
        spread = jnp.sum(buf[:, half:], axis=0) + each * jnp.sum(gap * gap, axis=0)
        return jnp.concatenate([mean, spread], axis=0)

    mid[...] = merge(near_buf, nears, float(points))
    for k in range(1, fars):
        pltpu.make_async_remote_copy(
            mid, far_buf.at[far], sems.at[2], sems.at[3],
            device_id=far_dev(r, x, (far + k) % fars), device_id_type=MESH,
        ).start()
    far_buf[far] = mid[...]
    take_some(far_buf, fars - 1, sems.at[3])
    take_some(far_buf, fars - 1, sems.at[2])
    out_ref[...] = merge(far_buf, fars, float(points * nears))


def exchange_moments(first, second, mode, points, collective_id):
    rows, cols = lax.axis_size("rows"), lax.axis_size("cols")
    width = first.shape[0]
    lines = width // 128
    packed = jnp.concatenate([first.reshape(lines, 128), second.reshape(lines, 128)], axis=0)
    merged = pl.pallas_call(
        functools.partial(moments_kernel, mode, points, rows, cols),
        out_shape=jax.ShapeDtypeStruct(packed.shape, F32),
        in_specs=[pl.BlockSpec(memory_space=pltpu.VMEM)],
        out_specs=pl.BlockSpec(memory_space=pltpu.VMEM),
        scratch_shapes=[
            pltpu.VMEM((rows * NEAR_X,) + packed.shape, F32),
            pltpu.VMEM((cols // NEAR_X,) + packed.shape, F32),
            pltpu.VMEM(packed.shape, F32),
            pltpu.SemaphoreType.DMA((4,)),
        ],
        compiler_params=pltpu.CompilerParams(collective_id=collective_id, has_side_effects=True),
        name="moments_" + mode,
    )(packed)
    return merged[:lines].reshape(width), merged[lines:].reshape(width)


def total_kernel(rows, cols, in_ref, out_ref, near_buf, far_buf, share, piece, sems):
    r, x, far, fars, near, nears = group_ids(rows, cols)
    greet(near, nears, far, fars, r, x)
    for k in range(1, nears):
        peer = (near + k) % nears
        pltpu.make_async_remote_copy(
            in_ref.at[peer], near_buf.at[near], sems.at[0], sems.at[1],
            device_id=near_dev(peer, far), device_id_type=MESH,
        ).start()
    near_buf[near] = in_ref[near]
    take_some(near_buf, nears - 1, sems.at[1])
    share[...] = jnp.sum(near_buf[...], axis=0)
    for k in range(1, fars):
        peer = (far + k) % fars
        pltpu.make_async_remote_copy(
            share.at[peer], far_buf.at[far], sems.at[2], sems.at[3],
            device_id=far_dev(r, x, peer), device_id_type=MESH,
        ).start()
    far_buf[far] = share[far]
    take_some(far_buf, fars - 1, sems.at[3])
    piece[...] = jnp.sum(far_buf[...], axis=0)
    for k in range(1, fars):
        pltpu.make_async_remote_copy(
            piece, out_ref.at[near, far], sems.at[4], sems.at[5],
            device_id=far_dev(r, x, (far + k) % fars), device_id_type=MESH,
        ).start()
    out_ref[near, far] = piece[...]
    take_some(far_buf, fars - 1, sems.at[5])
    for k in range(1, nears):
        pltpu.make_async_remote_copy(
            out_ref.at[near], out_ref.at[near], sems.at[6], sems.at[7],
            device_id=near_dev((near + k) % nears, far), device_id_type=MESH,
        ).start()
    take_some(near_buf, nears - 1, sems.at[7])
    take_some(near_buf, nears - 1, sems.at[0])
    take_some(far_buf, fars - 1, sems.at[2])
    take_some(far_buf, fars - 1, sems.at[4])
    take_some(near_buf, nears - 1, sems.at[6])


def sum_everywhere(value, collective_id):
    rows, cols = lax.axis_size("rows"), lax.axis_size("cols")
    nears, fars = rows * NEAR_X, cols // NEAR_X
    taps, width = value.shape
    lines = -(-(taps * width) // (nears * fars * 128))
    flat = jnp.pad(value.reshape(-1, 128), ((0, nears * fars * lines - taps * width // 128), (0, 0)))
    parts = flat.reshape(nears, fars, lines, 128)
    total = pl.pallas_call(
        functools.partial(total_kernel, rows, cols),
        out_shape=jax.ShapeDtypeStruct(parts.shape, F32),
        in_specs=[pl.BlockSpec(memory_space=pltpu.VMEM)],
        out_specs=pl.BlockSpec(memory_space=pltpu.VMEM),
        scratch_shapes=[
            pltpu.VMEM((nears, fars, lines, 128), F32),
            pltpu.VMEM((fars, lines, 128), F32),
            pltpu.VMEM((fars, lines, 128), F32),
            pltpu.VMEM((lines, 128), F32),
            pltpu.SemaphoreType.DMA((8,)),
        ],
        compiler_params=pltpu.CompilerParams(collective_id=collective_id, has_side_effects=True),
        name="kernel_total",
    )(parts)
    return total.reshape(-1, 128)[: taps * width // 128].reshape(taps, width)


def rim_pixels(block, radius):
    rows, cols = lax.axis_size("rows"), lax.axis_size("cols")
    down = [(i, i + 1) for i in range(rows - 1)]
    up = [(b, a) for a, b in down]
    east = [(i, i + 1) for i in range(cols - 1)]
    west = [(b, a) for a, b in east]
    top = lax.ppermute(block[-radius:], "rows", down)
    bottom = lax.ppermute(block[:radius], "rows", up)
    channel_count = block.shape[-1]

    def strip(sel):
        return jnp.concatenate([top[:, sel], block[:, sel], bottom[:, sel]], axis=0)

    left = lax.ppermute(strip(slice(-GROUP, None)), "cols", east)
    right = lax.ppermute(strip(slice(0, GROUP)), "cols", west)
    pieces = [top, bottom, left[radius:-radius], right[radius:-radius]]
    pieces += [left[:radius], right[:radius], left[-radius:], right[-radius:]]
    return jnp.concatenate([p.reshape(-1, channel_count) for p in pieces], axis=0)


def per_device(
    features,
    dw_kernel,
    batchnorm_gain,
    batchnorm_offset,
    w_in,
    b_in,
    w_out,
    b_out,
    layer_scale,
    w_down,
    b_down,
    cotangent,
):
    tile_height, tile_width, channel_count = features.shape
    radius = (dw_kernel.shape[0] - 1) // 2
    pixel_total = tile_height * lax.axis_size("rows") * tile_width * lax.axis_size("cols")
    pixels = tile_height * tile_width
    inner_t, rim_t, tap_t, out_t, tap_o = dft_tables(tile_height, tile_width, radius)
    half = HALF
    conv_out, feat_spec, moments, out_grad = forward_part(features, cotangent, dw_kernel, w_down)
    feat_re, feat_im = feat_spec[:half], feat_spec[half:]
    area = (tile_height + 2 * radius) * (tile_width + 2 * radius)

    def pixels_of(real, imag, table):
        spec = jnp.concatenate([real, imag], axis=0).astype(jnp.bfloat16)
        return fdot(table, spec) * (1.0 / area)

    taps = jnp.pad(dw_kernel.reshape(-1, channel_count), ((0, 87), (0, 0)))
    tap_spec = fdot(tap_t, taps)
    tap_re, tap_im = tap_spec[:half], tap_spec[half:]
    lines = channel_count // 128
    mean_val = moments[:lines].reshape(channel_count)
    variance = moments[lines:].reshape(channel_count) / pixel_total
    inverse_deviation = lax.rsqrt(variance + 1e-05)
    standardized_input = (conv_out - mean_val) * inverse_deviation
    normalized_input = (
        (standardized_input * batchnorm_gain + batchnorm_offset)
        .astype(jnp.bfloat16)
    )
    pre_act = jnp.dot(normalized_input, w_in, preferred_element_type=jnp.float32) + b_in
    activated = jax.nn.gelu(pre_act).astype(jnp.bfloat16)
    branch = jnp.dot(activated, w_out, preferred_element_type=jnp.float32) + b_out
    flat_feat = features.reshape(tile_height * tile_width, channel_count).astype(jnp.float32)
    summed = (flat_feat + layer_scale * branch).astype(jnp.bfloat16)
    blocks = summed.reshape(tile_height // 2, 2, tile_width // 2, 2, channel_count)
    local_coarse = (
        jnp.einsum("paqbc,abco->opq", blocks, w_down, preferred_element_type=jnp.float32)
        + b_down[:, None, None]
    )
    coarse = lax.all_to_all(
        local_coarse.astype(jnp.bfloat16), "cols", split_axis=0, concat_axis=2, tiled=True
    )
    scaled_grad = (layer_scale * out_grad.astype(jnp.float32)).astype(jnp.bfloat16)
    act_grad = jnp.dot(scaled_grad, w_out.T, preferred_element_type=jnp.float32)
    _, pullback = jax.vjp(jax.nn.gelu, pre_act)
    pre_grad = pullback(act_grad)[0].astype(jnp.bfloat16)
    normalized_gradient = jnp.dot(pre_grad, w_in.T, preferred_element_type=jnp.float32)
    standardized_gradient = normalized_gradient * batchnorm_gain
    gradient_total, gradient_product_sum = exchange_moments(
        jnp.sum(standardized_gradient, axis=0),
        jnp.sum(standardized_gradient * standardized_input, axis=0),
        "sum", pixels, 2,
    )
    convolution_gradient = (
        inverse_deviation
        * (
            standardized_gradient
            - gradient_total / pixel_total
            - standardized_input * (gradient_product_sum / pixel_total)
        )
    ).astype(jnp.bfloat16)
    grad_inner = fdot(inner_t, convolution_gradient)
    own_re, own_im = grad_inner[:half], grad_inner[half:]
    kernel_term = pixels_of(
        feat_re * own_re + feat_im * own_im, feat_im * own_re - feat_re * own_im, tap_o[:169]
    )
    grad_kernel = sum_everywhere(kernel_term, 3) * lax.rsqrt(jnp.float32(pixel_total))
    grad_kernel = grad_kernel.reshape(dw_kernel.shape)
    rim = rim_pixels(
        convolution_gradient.reshape(tile_height, tile_width, channel_count), radius
    )
    grad_spec = grad_inner + fdot(rim_t, rim)
    grad_re, grad_im = grad_spec[:half], grad_spec[half:]
    back_conv = pixels_of(
        grad_re * tap_re - grad_im * tap_im, grad_re * tap_im + grad_im * tap_re, out_t
    )
    grad_input = (
        (out_grad.astype(jnp.float32) + back_conv)
        .astype(jnp.bfloat16)
        .reshape(tile_height, tile_width, channel_count)
    )
    return (coarse, grad_input, grad_kernel)


def solution(mesh):
    in_specs = (
        P("rows", "cols", None),
        P(),
        P(),
        P(),
        P(),
        P(),
        P(),
        P(),
        P(),
        P(),
        P(),
        P("cols", "rows", None),
    )
    out_specs = (P("cols", "rows", None), P("rows", "cols", None), P())
    return jax.shard_map(
        per_device, mesh=mesh, in_specs=in_specs, out_specs=out_specs, check_vma=False
    )
```

```python
import functools

import jax
import jax.numpy as jnp
import numpy as np
from jax import lax
from jax.experimental import pallas as pl
from jax.experimental.pallas import tpu as pltpu
from jax.sharding import PartitionSpec as P

MESH = pl.DeviceIdType.MESH
F32 = jnp.float32
BF16 = jnp.bfloat16
NEAR_X = 4
GROUP = 8
HALF = 1024
TAP_LINE = 16
TAP_TILES = 7
TAP_ROWS = 4 * TAP_TILES * 8
GELU_A, GELU_B = 0.7978845608028654, 0.044715
CHUNK = 256


def balanced(table):
    low = table.astype(jnp.bfloat16)
    bits = low.view(np.uint16)
    up = (bits + 1).astype(np.uint16).view(jnp.bfloat16).astype(np.float64)
    down = (bits - 1).astype(np.uint16).view(jnp.bfloat16).astype(np.float64)
    value = low.astype(np.float64)
    out = value.copy()
    for row in range(table.shape[0]):
        excess = (value[row] - table[row]).sum()
        if excess == 0.0:
            continue
        live = np.nonzero(np.abs(table[row]) > 0.004)[0]
        steps = np.stack([up[row, live], down[row, live]]) - value[row, live]
        order = np.argsort(-np.abs(steps[0]), kind="stable")
        for spot in order:
            for step in steps[:, spot]:
                if abs(excess + step) < abs(excess) - 0.25 * abs(step):
                    out[row, live[spot]] += step
                    excess += step
                    break
    return out.astype(jnp.bfloat16)


@functools.lru_cache(maxsize=None)
def dft_tables(tile_h, tile_w, radius):
    nh, nw = tile_h + 2 * radius, tile_w + 2 * radius
    u, v, weight = np.zeros(HALF), np.zeros(HALF), np.zeros(HALF)
    index = 0
    for a in range(nh):
        for b in range(nw // 2 + 1):
            edge = b in (0, nw // 2)
            if edge and a > nh // 2:
                continue
            u[index], v[index] = a, b
            weight[index] = 1.0 if edge and a in (0, nh // 2) else 2.0
            index += 1
    live = weight > 0

    def rows(points):
        p = np.asarray(points)
        turns = (np.outer(u, p[:, 0]) % nh) / nh + (np.outer(v, p[:, 1]) % nw) / nw
        angle = 2.0 * np.pi * turns
        table = np.concatenate([np.cos(angle) * live[:, None], -np.sin(angle) * live[:, None]])
        table[np.abs(table) < 1e-9] = 0.0
        return table

    inner = [(h, w) for h in range(tile_h) for w in range(tile_w)]
    wests = range(-GROUP, 0)
    easts = range(tile_w, tile_w + GROUP)
    norths = range(-radius, 0)
    souths = range(tile_h, tile_h + radius)
    rim = [(h, w) for hs in (norths, souths) for h in hs for w in range(tile_w)]
    rim += [(h, w) for ws in (wests, easts) for h in range(tile_h) for w in ws]
    rim += [(h, w) for hs in (norths, souths) for ws in (wests, easts) for h in hs for w in ws]
    kept = np.asarray([-radius <= w < tile_w + radius for _, w in rim])
    taps = [(i, j) for i in range(-radius, radius + 1) for j in range(-radius, radius + 1)]
    both = balanced(np.concatenate([rows(inner), rows(rim) * kept[None]], axis=1))
    count = len(inner)
    spot = [(i + radius) * TAP_LINE + j + radius for i, j in taps]
    doubled = np.concatenate([weight, weight])[None]
    f_tap = np.zeros((2 * HALF, CHUNK))
    f_tap[:, spot] = rows(taps)
    g_tap = np.zeros((TAP_ROWS, 2 * HALF))
    g_tap[spot] = rows(taps).T * doubled
    f_tap, g_tap = f_tap.astype(jnp.bfloat16), g_tap.astype(jnp.bfloat16)
    f_out = (rows(inner).T * doubled).astype(jnp.bfloat16)
    return both[:, :count], both[:, count:], f_tap, f_out, g_tap


@functools.lru_cache(maxsize=None)
def phase_table(tile_w):
    table = np.zeros((CHUNK, CHUNK), np.float32)
    lines = CHUNK // tile_w
    for h in range(lines):
        for w in range(tile_w):
            plane = (h % 2) * 2 + w % 2
            table[plane * 64 + (h // 2) * (tile_w // 2) + w // 2, h * tile_w + w] = 1.0
    return table.astype(jnp.bfloat16)


def fdot(a, b):
    return jnp.dot(a, b, preferred_element_type=F32)


def ndot(a, b):
    return lax.dot_general(a, b, (((1,), (1,)), ((), ())), preferred_element_type=F32)


def rows_of(step, size=CHUNK):
    return pl.ds(pl.multiple_of(step * size, size), size)


def swap_blocks(parts):
    lane = lax.broadcasted_iota(jnp.int32, parts[0].shape, 1) // 16
    parts = list(parts)
    for k in (1, 2, 4):
        low = (lane // k) % 2 == 0
        for i in range(8):
            if i & k:
                continue
            a, b = parts[i], parts[i | k]
            parts[i] = jnp.where(low, a, pltpu.roll(b, 16 * k, 1))
            parts[i | k] = jnp.where(low, pltpu.roll(a, 128 - 16 * k, 1), b)
    return parts


class Place:
    def __init__(self, rows, cols):
        self.rows, self.cols = rows, cols
        self.r, self.c = lax.axis_index("rows"), lax.axis_index("cols")
        self.x, self.far = self.c % NEAR_X, self.c // NEAR_X
        self.fars, self.nears = cols // NEAR_X, rows * NEAR_X
        self.near = self.r * NEAR_X + self.x

    def near_dev(self, k):
        peer = (self.near + k) % self.nears
        return peer, {"rows": peer // NEAR_X, "cols": self.far * NEAR_X + peer % NEAR_X}

    def far_dev(self, k):
        peer = (self.far + k) % self.fars
        return peer, {"rows": self.r, "cols": peer * NEAR_X + self.x}

    def col_dev(self, k):
        peer = (self.c + k) % self.cols
        return peer, {"rows": self.r, "cols": peer}

    def inside(self, dr, dc):
        r, c = self.r + dr, self.c + dc
        return (r >= 0) & (r < self.rows) & (c >= 0) & (c < self.cols)

    def rim_dev(self, dr, dc):
        return {"rows": self.r + dr, "cols": self.c + dc}

    def greet(self):
        barrier = pltpu.get_barrier_semaphore()
        for dr, dc in STEPS:
            @pl.when(self.inside(dr, dc))
            def _():
                pl.semaphore_signal(
                    barrier, inc=1, device_id=self.rim_dev(dr, dc), device_id_type=MESH
                )
        for count, dev in (
            (self.nears, self.near_dev), (self.fars, self.far_dev), (self.cols, self.col_dev)
        ):
            for k in range(1, count):
                pl.semaphore_signal(barrier, inc=1, device_id=dev(k)[1], device_id_type=MESH)

    def met(self):
        def beside(at, size):
            return 1 + (at + size - 1) // size + (2 * size - 2 - at) // size

        around = beside(self.r, self.rows) * beside(self.c, self.cols) - 1
        pl.semaphore_wait(
            pltpu.get_barrier_semaphore(), around + self.nears + self.fars + self.cols - 3
        )


STEPS = ((1, 0), (-1, 0), (0, 1), (0, -1), (1, 1), (1, -1), (-1, 1), (-1, -1))


def send(src, dst, sems, slot, dev):
    pltpu.make_async_remote_copy(
        src, dst, sems.at[slot], sems.at[slot + 1], device_id=dev, device_id_type=MESH
    ).start()


def take(ref, sem):
    pltpu.make_async_copy(ref, ref, sem).wait()


def rim_pieces(block, radius, tb, lr, corner):
    lines, groups = block.shape[0], block.shape[1]
    south, north = pl.ds(lines - radius, radius), pl.ds(0, radius)
    last = groups - 1
    return (
        (block.at[south], tb.at[0]),
        (block.at[north], tb.at[1]),
        (block.at[:, last], lr.at[0]),
        (block.at[:, 0], lr.at[1]),
        (block.at[south, last], corner.at[0]),
        (block.at[south, 0], corner.at[1]),
        (block.at[north, last], corner.at[2]),
        (block.at[north, 0], corner.at[3]),
    )


def start_rim(place, pieces, sems):
    for (dr, dc), (src, dst), k in zip(STEPS, pieces, range(8)):
        @pl.when(place.inside(dr, dc))
        def _():
            send(src, dst, sems, 2 * k, place.rim_dev(dr, dc))


def finish_rim(place, pieces, sems, tb, lr, corner, rim):
    for (dr, dc), (_, dst), k in zip(STEPS, pieces, range(8)):
        @pl.when(place.inside(-dr, -dc))
        def _():
            take(dst, sems.at[2 * k + 1])

        @pl.when(jnp.logical_not(place.inside(-dr, -dc)))
        def _():
            dst[...] = jnp.zeros(dst.shape, BF16)

    channels = rim.shape[1]
    at = 0
    for ref in (tb, lr, corner):
        count = int(np.prod(ref.shape[:-1]))
        flat = ref[...].astype(F32).reshape(count, channels).astype(BF16)
        rim[at : at + count] = flat
        at += count


def drain_rim(place, pieces, sems):
    for (dr, dc), (_, dst), k in zip(STEPS, pieces, range(8)):
        @pl.when(place.inside(dr, dc))
        def _():
            take(dst, sems.at[2 * k])


def lines_of(row):
    return jnp.concatenate([row[:, k * 128 : (k + 1) * 128] for k in range(row.shape[1] // 128)], 0)


def row_of(lines):
    return jnp.concatenate([lines[k : k + 1] for k in range(lines.shape[0])], 1)


def merge_moments(buf, count, each):
    half = buf.shape[1] // 2
    means = buf[:, :half]
    mean = jnp.sum(means, axis=0) * (1.0 / count)
    gap = means - mean[None]
    spread = jnp.sum(buf[:, half:], axis=0) + each * jnp.sum(gap * gap, axis=0)
    return jnp.concatenate([mean, spread], axis=0)


def step_kernel(
    rows, cols, radius,
    feat_hbm, feat4_hbm, cot_hbm, tap_hbm, fin_hbm, frim_hbm, ftap_hbm, fout_hbm, gtap_hbm,
    down_hbm, phase_hbm, win_hbm, wout_hbm, gain, offset, b_in, b_out, scale, b_down,
    coarse_ref, grad_in_ref, grad_tap_ref,
    feat, cot, tap_raw, fin, frim, ftap, fout, gtap, down, phase, win, wout,
    cot32, spread, cot_in, coarse_in, taps, tap_spec, mixed, spec, own, conv, grad, xgrad, act,
    tb, lr, corner, rim, planes, edge,
    near_buf, far_buf, near_sum, far_sum, mine, mid, sums, sums_mid,
    tap_part, tap_near, tap_share, tap_far, tap_piece, tap_all,
    in_sems, rim_sems, sems,
):
    place = Place(rows, cols)
    sources = (
        (cot_hbm, cot), (tap_hbm, tap_raw), (ftap_hbm, ftap), (feat_hbm, feat), (fin_hbm, fin),
        (frim_hbm, frim), (fout_hbm, fout), (down_hbm, down), (phase_hbm, phase),
        (win_hbm, win), (wout_hbm, wout), (gtap_hbm, gtap),
    )
    loads = [
        pltpu.make_async_copy(src, dst, in_sems.at[k]) for k, (src, dst) in enumerate(sources)
    ]
    for load in loads:
        load.start()
    place.greet()

    outs, lines, width = cot.shape
    pixels, channels = conv.shape
    side = pixels // (2 * lines)
    parts_n = pixels // CHUNK
    area = (2 * lines + 2 * radius) * (side + 2 * radius)
    everything = float(pixels * rows * cols)
    zero = jnp.zeros((1, channels), F32)

    loads[0].wait()
    for tg in range(width // 128):
        cot32[tg] = cot[:, :, tg * 128 : (tg + 1) * 128].astype(F32).reshape(outs * lines, 128)
        for pg in range(lines // 8):
            parts = swap_blocks([
                cot32[tg, pl.ds(pg * 8 + k, outs, stride=lines), :] for k in range(8)
            ])
            for k in range(8):
                spread[tg * 8 + k, :, pg * 128 : (pg + 1) * 128] = parts[k].astype(BF16)
    place.met()
    pieces = rim_pieces(feat4_hbm, radius, tb, lr, corner)
    start_rim(place, pieces, rim_sems)
    for k in range(1, cols):
        peer, dev = place.col_dev(k)
        send(spread.at[peer], cot_in.at[place.c], sems, 0, dev)
    cot_in[place.c] = spread[place.c]

    loads[1].wait()
    loads[2].wait()
    taps[...] = jnp.zeros(taps.shape, BF16)
    for i in range(2 * radius + 1):
        taps[i * TAP_LINE : i * TAP_LINE + 2 * radius + 1] = tap_raw[i]

    @pl.loop(0, 2 * HALF // CHUNK)
    def _(m):
        tap_spec[rows_of(m)] = fdot(ftap[rows_of(m)], taps[...])

    loads[3].wait()
    loads[4].wait()

    @pl.loop(0, 2 * HALF // CHUNK)
    def _(m):
        spec[rows_of(m)] = fdot(fin[rows_of(m)], feat[...])

    finish_rim(place, pieces, rim_sems, tb, lr, corner, rim)
    loads[5].wait()

    @pl.loop(0, HALF // CHUNK)
    def _(m):
        re, im = rows_of(m), rows_of(m + HALF // CHUNK)
        fr = spec[re] + fdot(frim[re], rim[...])
        fi = spec[im] + fdot(frim[im], rim[...])
        spec[re], spec[im] = fr, fi
        kr, ki = tap_spec[re], tap_spec[im]
        mixed[re] = (fr * kr + fi * ki).astype(BF16)
        mixed[im] = (fi * kr - fr * ki).astype(BF16)

    loads[6].wait()

    def invert(m, total):
        block = fdot(fout[rows_of(m)], mixed[...]) * (1.0 / area)
        conv[rows_of(m)] = block
        return total + jnp.sum(block, axis=0, keepdims=True)

    local = lax.fori_loop(0, parts_n, invert, zero) * (1.0 / pixels)

    def scatter(m, total):
        gap = conv[rows_of(m)] - local
        return total + jnp.sum(gap * gap, axis=0, keepdims=True)

    around = lax.fori_loop(0, parts_n, scatter, zero)
    mine[...] = jnp.concatenate([lines_of(local), lines_of(around)], axis=0)
    for k in range(1, place.nears):
        send(mine, near_buf.at[place.near], sems, 2, place.near_dev(k)[1])
    near_buf[place.near] = mine[...]

    take(cot_in.at[pl.ds(0, cols - 1)], sems.at[1])
    loads[7].wait()
    loads[8].wait()
    tall = cot_in[...].reshape(cols * outs, lines * lines).astype(F32).T.astype(BF16)
    for ab in range(4):
        planes[ab] = ndot(tall, down[ab]).astype(BF16)
    take(near_buf.at[pl.ds(0, place.nears - 1)], sems.at[3])
    mid[...] = merge_moments(near_buf, place.nears, float(pixels))
    for k in range(1, place.fars):
        send(mid, far_buf.at[place.far], sems, 4, place.far_dev(k)[1])
    far_buf[place.far] = mid[...]
    for k in range(parts_n):
        block = jnp.concatenate([planes[ab, k * 64 : (k + 1) * 64] for ab in range(4)], axis=0)
        grad[k * CHUNK : (k + 1) * CHUNK] = lax.dot_general(
            phase[...], block, (((0,), (0,)), ((), ())), preferred_element_type=F32
        ).astype(BF16)
    take(far_buf.at[pl.ds(0, place.fars - 1)], sems.at[5])
    moments = merge_moments(far_buf, place.fars, float(pixels * place.nears))
    take(cot_in.at[pl.ds(0, cols - 1)], sems.at[0])
    drain_rim(place, pieces, rim_sems)

    half = moments.shape[0] // 2
    mean = row_of(moments[:half])
    inverse = lax.rsqrt(row_of(moments[half:]) * (1.0 / everything) + 1e-05)
    loads[9].wait()
    loads[10].wait()
    hidden = win.shape[1]
    step = 512

    def mlp(m, totals):
        at = rows_of(m)
        xhat = (conv[at] - mean) * inverse
        normed = (xhat * gain[...] + offset[...]).astype(BF16)
        scaled = (scale[...] * grad[at].astype(F32)).astype(BF16)
        back = jnp.zeros((CHUNK, channels), F32)
        for j in range(hidden // step):
            cut = slice(j * step, (j + 1) * step)
            v = fdot(normed, win[:, cut]) + b_in[:, cut]
            act_grad = ndot(scaled, wout[cut])
            square = v * v
            t = jnp.tanh(GELU_A * v * (1.0 + GELU_B * square))
            gate = 0.5 * (1.0 + t)
            act[at, cut] = (v * gate).astype(BF16)
            slope = gate + (0.5 * GELU_A) * v * (1.0 - t * t) * (1.0 + (3.0 * GELU_B) * square)
            back = back + ndot((act_grad * slope).astype(BF16), win[:, cut])
        back = back * gain[...]
        xgrad[at] = back
        return (
            totals[0] + jnp.sum(back, axis=0, keepdims=True),
            totals[1] + jnp.sum(back * xhat, axis=0, keepdims=True),
        )

    total, product = lax.fori_loop(0, parts_n, mlp, (zero, zero))
    sums[...] = jnp.concatenate([lines_of(total), lines_of(product)], axis=0)
    for k in range(1, place.nears):
        send(sums, near_sum.at[place.near], sems, 6, place.near_dev(k)[1])
    near_sum[place.near] = sums[...]

    for k in range(parts_n):
        at = slice(k * CHUNK, (k + 1) * CHUNK)
        branch = fdot(act[at], wout[...]) + b_out[...]
        summed = (feat[at].astype(F32) + scale[...] * branch).astype(BF16)
        split = fdot(phase[...], summed).astype(BF16)
        for ab in range(4):
            planes[ab, k * 64 : (k + 1) * 64] = split[ab * 64 : (ab + 1) * 64]
    take(near_sum.at[pl.ds(0, place.nears - 1)], sems.at[7])
    sums_mid[...] = jnp.sum(near_sum[...], axis=0)
    for k in range(1, place.fars):
        send(sums_mid, far_sum.at[place.far], sems, 8, place.far_dev(k)[1])
    far_sum[place.far] = sums_mid[...]
    flat = b_down[...]
    for ab in range(4):
        flat = flat + fdot(planes[ab], down[ab])
    spread[...] = flat.T.astype(BF16).reshape(cols, outs, lines * lines)
    for k in range(1, cols):
        peer, dev = place.col_dev(k)
        send(spread.at[peer], coarse_in.at[place.c], sems, 10, dev)
    coarse_in[place.c] = spread[place.c]
    take(far_sum.at[pl.ds(0, place.fars - 1)], sems.at[9])
    both = jnp.sum(far_sum[...], axis=0) * (1.0 / everything)
    level, slant = row_of(both[:half]), row_of(both[half:])

    groups = edge.shape[1]
    for k in range(parts_n):
        at = slice(k * CHUNK, (k + 1) * CHUNK)
        xhat = (conv[at] - mean) * inverse
        block = inverse * (xgrad[at] - level - xhat * slant)
        feat[at] = block.astype(BF16)
        tall_lines = CHUNK // side
        edge[k * tall_lines : (k + 1) * tall_lines] = block.reshape(
            tall_lines, groups, GROUP, channels
        ).astype(BF16)
    pieces = rim_pieces(edge, radius, tb, lr, corner)
    start_rim(place, pieces, rim_sems)

    @pl.loop(0, HALF // CHUNK)
    def _(m):
        re, im = rows_of(m), rows_of(m + HALF // CHUNK)
        gr, gi = fdot(fin[re], feat[...]), fdot(fin[im], feat[...])
        own[re], own[im] = gr, gi
        fr, fi = spec[re], spec[im]
        mixed[re] = (fr * gr + fi * gi).astype(BF16)
        mixed[im] = (fi * gr - fr * gi).astype(BF16)

    loads[11].wait()
    norm = 1.0 / (area * float(np.sqrt(everything)))
    tap_part[...] = (fdot(gtap[...], mixed[...]) * norm).reshape(tap_part.shape)

    def tap_block(index):
        start = pl.multiple_of((index % NEAR_X) * 128, 128)
        return tap_part.at[pl.ds((index // NEAR_X) * TAP_TILES, TAP_TILES), :, pl.ds(start, 128)]

    for k in range(1, place.nears):
        peer, dev = place.near_dev(k)
        send(tap_block(peer), tap_near.at[place.near], sems, 12, dev)
    tap_near[place.near] = tap_block(place.near)[...]

    finish_rim(place, pieces, rim_sems, tb, lr, corner, rim)

    @pl.loop(0, HALF // CHUNK)
    def _(m):
        re, im = rows_of(m), rows_of(m + HALF // CHUNK)
        gr = own[re] + fdot(frim[re], rim[...])
        gi = own[im] + fdot(frim[im], rim[...])
        kr, ki = tap_spec[re], tap_spec[im]
        mixed[re] = (gr * kr - gi * ki).astype(BF16)
        mixed[im] = (gr * ki + gi * kr).astype(BF16)

    take(tap_near.at[pl.ds(0, place.nears - 1)], sems.at[13])
    tap_share[...] = jnp.sum(tap_near[...], axis=0)
    owner = place.far < TAP_TILES
    for k in range(1, place.fars):
        peer, dev = place.far_dev(k)

        @pl.when(peer < TAP_TILES)
        def _():
            send(tap_share.at[peer], tap_far.at[place.far], sems, 14, dev)

    def spread_out(m):
        at = slice(m * CHUNK, (m + 1) * CHUNK)
        block = fdot(fout[at], mixed[...]) * (1.0 / area)
        grad_in_ref[at] = (grad[at].astype(F32) + block).astype(BF16)

    for m in range(parts_n // 2):
        spread_out(m)

    @pl.when(owner)
    def _():
        tap_far[place.far] = tap_share[place.far]
        take(tap_far.at[pl.ds(0, place.fars - 1)], sems.at[15])
        tap_piece[...] = jnp.sum(tap_far[...], axis=0)
        for k in range(1, place.fars):
            send(tap_piece, tap_all.at[place.near, place.far], sems, 16, place.far_dev(k)[1])
        tap_all[place.near, place.far] = tap_piece[...]

    for m in range(parts_n // 2, parts_n):
        spread_out(m)

    @pl.when(owner)
    def _():
        take(tap_far.at[pl.ds(0, TAP_TILES - 1)], sems.at[17])
        take(tap_far.at[pl.ds(0, TAP_TILES - 1)], sems.at[14])
        take(tap_far.at[pl.ds(0, place.fars - 1)], sems.at[16])

    @pl.when(jnp.logical_not(owner))
    def _():
        take(tap_far.at[pl.ds(0, TAP_TILES)], sems.at[17])
        take(tap_far.at[pl.ds(0, TAP_TILES)], sems.at[14])

    for k in range(1, place.nears):
        send(tap_all.at[place.near], tap_all.at[place.near], sems, 18, place.near_dev(k)[1])

    take(coarse_in.at[pl.ds(0, cols - 1)], sems.at[11])
    for tg in range(width // 128):
        for pg in range(lines // 8):
            parts = swap_blocks([
                coarse_in[tg * 8 + k, :, pg * 128 : (pg + 1) * 128].astype(F32) for k in range(8)
            ])
            for k in range(8):
                cot32[tg, pl.ds(pg * 8 + k, outs, stride=lines), :] = parts[k]
        coarse_ref[:, :, tg * 128 : (tg + 1) * 128] = (
            cot32[tg].reshape(outs, lines, 128).astype(BF16)
        )
    take(tap_near.at[pl.ds(0, place.nears - 1)], sems.at[19])
    for i in range(2 * radius + 1):
        for b in range(NEAR_X):
            tile = [
                tap_all[(g // TAP_TILES) * NEAR_X + b, g % TAP_TILES] for g in (2 * i, 2 * i + 1)
            ]
            line = jnp.concatenate(tile, axis=0)[: 2 * radius + 1]
            grad_tap_ref[i, :, b * 128 : (b + 1) * 128] = line
    drain_rim(place, pieces, rim_sems)
    take(near_buf.at[pl.ds(0, place.nears - 1)], sems.at[2])
    take(far_buf.at[pl.ds(0, place.fars - 1)], sems.at[4])
    take(near_sum.at[pl.ds(0, place.nears - 1)], sems.at[6])
    take(far_sum.at[pl.ds(0, place.fars - 1)], sems.at[8])
    take(coarse_in.at[pl.ds(0, cols - 1)], sems.at[10])
    take(tap_near.at[pl.ds(0, place.nears - 1)], sems.at[12])
    take(tap_near.at[pl.ds(0, place.nears - 1)], sems.at[18])


def per_device(
    features, dw_kernel, batchnorm_gain, batchnorm_offset, w_in, b_in, w_out, b_out,
    layer_scale, w_down, b_down, cotangent,
):
    rows, cols = lax.axis_size("rows"), lax.axis_size("cols")
    tile_h, tile_w, channels = features.shape
    radius = (dw_kernel.shape[0] - 1) // 2
    pixels = tile_h * tile_w
    tables = [jnp.asarray(t) for t in dft_tables(tile_h, tile_w, radius)]
    groups = tile_w // GROUP
    outs, lines, width = cotangent.shape
    hidden = w_in.shape[1]
    far = (
        features.reshape(pixels, channels),
        features.reshape(tile_h, groups, GROUP, channels),
        cotangent,
        dw_kernel,
        *tables,
        w_down.reshape(4, channels, w_down.shape[-1]),
        jnp.asarray(phase_table(tile_w)),
        w_in,
        w_out,
    )
    near = tuple(
        v.reshape(1, -1)
        for v in (batchnorm_gain, batchnorm_offset, b_in, b_out, layer_scale, b_down)
    )
    stats = (2 * channels // 128, 128)
    nears, fars = rows * NEAR_X, cols // NEAR_X
    vm = pltpu.VMEM
    scratch = [vm(a.shape, BF16) for k, a in enumerate(far) if k != 1]
    scratch += [
        vm((width // 128, outs * lines, 128), F32),
        vm((cols, outs, lines * lines), BF16),
        vm((cols, outs, lines * lines), BF16),
        vm((cols, outs, lines * lines), BF16),
        vm((CHUNK, channels), BF16),
        vm((2 * HALF, channels), F32),
        vm((2 * HALF, channels), BF16),
        vm((2 * HALF, channels), F32),
        vm((2 * HALF, channels), F32),
        vm((pixels, channels), F32),
        vm((pixels, channels), BF16),
        vm((pixels, channels), F32),
        vm((pixels, hidden), BF16),
        vm((2, radius, groups, GROUP, channels), BF16),
        vm((2, tile_h, GROUP, channels), BF16),
        vm((4, radius, GROUP, channels), BF16),
        vm((tables[1].shape[1], channels), BF16),
        vm((4, pixels // 4, channels), BF16),
        vm((tile_h, groups, GROUP, channels), BF16),
        vm((nears,) + stats, F32),
        vm((fars,) + stats, F32),
        vm((nears,) + stats, F32),
        vm((fars,) + stats, F32),
        vm(stats, F32),
        vm(stats, F32),
        vm(stats, F32),
        vm(stats, F32),
        vm((TAP_ROWS // 8, 8, channels), F32),
        vm((nears, TAP_TILES, 8, 128), F32),
        vm((TAP_TILES, 8, 128), F32),
        vm((fars, 8, 128), F32),
        vm((8, 128), F32),
        vm((nears, TAP_TILES, 8, 128), F32),
        pltpu.SemaphoreType.DMA((12,)),
        pltpu.SemaphoreType.DMA((16,)),
        pltpu.SemaphoreType.DMA((20,)),
    ]
    coarse, grad_input, grad_kernel = pl.pallas_call(
        functools.partial(step_kernel, rows, cols, radius),
        out_shape=(
            jax.ShapeDtypeStruct(cotangent.shape, BF16),
            jax.ShapeDtypeStruct((pixels, channels), BF16),
            jax.ShapeDtypeStruct(dw_kernel.shape, F32),
        ),
        in_specs=[pl.BlockSpec(memory_space=pl.ANY)] * len(far)
        + [pl.BlockSpec(memory_space=pltpu.VMEM)] * len(near),
        out_specs=[pl.BlockSpec(memory_space=pltpu.VMEM)] * 3,
        scratch_shapes=scratch,
        compiler_params=pltpu.CompilerParams(
            collective_id=1, has_side_effects=True, vmem_limit_bytes=67043328
        ),
        name="step",
    )(*far, *near)
    return coarse, grad_input.reshape(features.shape), grad_kernel


def solution(mesh):
    in_specs = (
        P("rows", "cols", None),
        P(),
        P(),
        P(),
        P(),
        P(),
        P(),
        P(),
        P(),
        P(),
        P(),
        P("cols", "rows", None),
    )
    out_specs = (P("cols", "rows", None), P("rows", "cols", None), P())
    return jax.shard_map(
        per_device, mesh=mesh, in_specs=in_specs, out_specs=out_specs, check_vma=False
    )
```

```python
import functools

import jax
import jax.numpy as jnp
import numpy as np
from jax import lax
from jax.experimental import pallas as pl
from jax.experimental.pallas import tpu as pltpu
from jax.sharding import PartitionSpec as P

MESH = pl.DeviceIdType.MESH
F32 = jnp.float32
BF16 = jnp.bfloat16
NEAR_X = 4
CORNER = 48
HALF = 1024
TAP_LINE = 16
TAP_TILES = 4
TAP_ROWS = 4 * TAP_TILES * TAP_LINE
GELU_A, GELU_B = 0.7978845608028654, 0.044715
CHUNK = 256


def balanced(table):
    low = table.astype(jnp.bfloat16)
    bits = low.view(np.uint16)
    up = (bits + 1).astype(np.uint16).view(jnp.bfloat16).astype(np.float64)
    down = (bits - 1).astype(np.uint16).view(jnp.bfloat16).astype(np.float64)
    value = low.astype(np.float64)
    out = value.copy()
    for row in range(table.shape[0]):
        excess = (value[row] - table[row]).sum()
        if excess == 0.0:
            continue
        live = np.nonzero(np.abs(table[row]) > 0.004)[0]
        steps = np.stack([up[row, live], down[row, live]]) - value[row, live]
        order = np.argsort(-np.abs(steps[0]), kind="stable")
        for spot in order:
            for step in steps[:, spot]:
                if abs(excess + step) < abs(excess) - 0.25 * abs(step):
                    out[row, live[spot]] += step
                    excess += step
                    break
    return out.astype(jnp.bfloat16)


@functools.lru_cache(maxsize=None)
def dft_tables(tile_h, tile_w, radius):
    nh, nw = tile_h + 2 * radius, tile_w + 2 * radius
    u, v, weight = np.zeros(HALF), np.zeros(HALF), np.zeros(HALF)
    index = 0
    for a in range(nh):
        for b in range(nw // 2 + 1):
            edge = b in (0, nw // 2)
            if edge and a > nh // 2:
                continue
            u[index], v[index] = a, b
            weight[index] = 1.0 if edge and a in (0, nh // 2) else 2.0
            index += 1
    live = weight > 0

    def rows(points):
        p = np.asarray(points)
        turns = (np.outer(u, p[:, 0]) % nh) / nh + (np.outer(v, p[:, 1]) % nw) / nw
        angle = 2.0 * np.pi * turns
        table = np.concatenate([np.cos(angle) * live[:, None], -np.sin(angle) * live[:, None]])
        table[np.abs(table) < 1e-9] = 0.0
        return table

    inner = [(h, w) for h in range(tile_h) for w in range(tile_w)]
    wests = range(-radius, 0)
    easts = range(tile_w, tile_w + radius)
    norths = range(-radius, 0)
    souths = range(tile_h, tile_h + radius)
    rim = [(h, w) for hs in (norths, souths) for h in hs for w in range(tile_w)]
    rim += [(h, w) for ws in (wests, easts) for h in range(tile_h) for w in ws]
    kept = [True] * len(rim)
    for hs in (norths, souths):
        for ws in (wests, easts):
            part = [(h, w) for h in hs for w in ws]
            spare = CORNER - len(part)
            rim += part + [(0, 0)] * spare
            kept += [True] * len(part) + [False] * spare
    kept = np.asarray(kept, np.float64)
    taps = [(i, j) for i in range(-radius, radius + 1) for j in range(-radius, radius + 1)]
    both = balanced(np.concatenate([rows(inner), rows(rim) * kept[None]], axis=1))
    count = len(inner)
    spot = [(i + radius) * TAP_LINE + j + radius for i, j in taps]
    doubled = np.concatenate([weight, weight])[None]
    f_tap = np.zeros((2 * HALF, CHUNK))
    f_tap[:, spot] = rows(taps)
    g_tap = np.zeros((TAP_ROWS, 2 * HALF))
    g_tap[spot] = rows(taps).T * doubled
    f_tap, g_tap = f_tap.astype(jnp.bfloat16), g_tap.astype(jnp.bfloat16)
    f_out = (rows(inner).T * doubled).astype(jnp.bfloat16)
    return both[:, :count], both[:, count:], f_tap, f_out, g_tap


@functools.lru_cache(maxsize=None)
def phase_table(tile_w):
    table = np.zeros((CHUNK, CHUNK), np.float32)
    lines = CHUNK // tile_w
    for h in range(lines):
        for w in range(tile_w):
            plane = (h % 2) * 2 + w % 2
            table[plane * 64 + (h // 2) * (tile_w // 2) + w // 2, h * tile_w + w] = 1.0
    return table.astype(jnp.bfloat16)


@functools.lru_cache(maxsize=None)
def border_table(tile_h, tile_w, radius):
    first, last = range(radius), range(tile_w - radius, tile_w)
    top, bottom = range(radius), range(tile_h - radius, tile_h)
    picks = [(h, w) for ws in (last, first) for h in range(tile_h) for w in ws]
    for hs in (bottom, top):
        for ws in (last, first):
            part = [(h, w) for h in hs for w in ws]
            picks += part + [None] * (CORNER - len(part))
    table = np.zeros((len(picks), tile_h * tile_w), np.float32)
    for row, pick in enumerate(picks):
        if pick is not None:
            table[row, pick[0] * tile_w + pick[1]] = 1.0
    return table.astype(jnp.bfloat16)


def fdot(a, b):
    return jnp.dot(a, b, preferred_element_type=F32)


def ndot(a, b):
    return lax.dot_general(a, b, (((1,), (1,)), ((), ())), preferred_element_type=F32)


def rows_of(step, size=CHUNK):
    return pl.ds(pl.multiple_of(step * size, size), size)


def swap_blocks(parts):
    lane = lax.broadcasted_iota(jnp.int32, parts[0].shape, 1) // 16
    parts = list(parts)
    for k in (1, 2, 4):
        low = (lane // k) % 2 == 0
        for i in range(8):
            if i & k:
                continue
            a, b = parts[i], parts[i | k]
            parts[i] = jnp.where(low, a, pltpu.roll(b, 16 * k, 1))
            parts[i | k] = jnp.where(low, pltpu.roll(a, 128 - 16 * k, 1), b)
    return parts


class Place:
    def __init__(self, rows, cols):
        self.rows, self.cols = rows, cols
        self.r, self.c = lax.axis_index("rows"), lax.axis_index("cols")
        self.x, self.far = self.c % NEAR_X, self.c // NEAR_X
        self.fars, self.nears = cols // NEAR_X, rows * NEAR_X
        self.near = self.r * NEAR_X + self.x

    def near_dev(self, k):
        peer = (self.near + k) % self.nears
        return peer, {"rows": peer // NEAR_X, "cols": self.far * NEAR_X + peer % NEAR_X}

    def far_dev(self, k):
        peer = (self.far + k) % self.fars
        return peer, {"rows": self.r, "cols": peer * NEAR_X + self.x}

    def col_dev(self, k):
        peer = (self.c + k) % self.cols
        return peer, {"rows": self.r, "cols": peer}

    def inside(self, dr, dc):
        r, c = self.r + dr, self.c + dc
        return (r >= 0) & (r < self.rows) & (c >= 0) & (c < self.cols)

    def rim_dev(self, dr, dc):
        return {"rows": self.r + dr, "cols": self.c + dc}

    def greet(self):
        barrier = pltpu.get_barrier_semaphore()
        for dr, dc in STEPS:
            @pl.when(self.inside(dr, dc))
            def _():
                pl.semaphore_signal(
                    barrier, inc=1, device_id=self.rim_dev(dr, dc), device_id_type=MESH
                )
        for count, dev in (
            (self.nears, self.near_dev), (self.fars, self.far_dev), (self.cols, self.col_dev)
        ):
            for k in range(1, count):
                pl.semaphore_signal(barrier, inc=1, device_id=dev(k)[1], device_id_type=MESH)

    def met(self):
        def beside(at, size):
            return 1 + (at + size - 1) // size + (2 * size - 2 - at) // size

        around = beside(self.r, self.rows) * beside(self.c, self.cols) - 1
        pl.semaphore_wait(
            pltpu.get_barrier_semaphore(), around + self.nears + self.fars + self.cols - 3
        )


STEPS = ((1, 0), (-1, 0), (0, 1), (0, -1), (1, 1), (1, -1), (-1, 1), (-1, -1))


def send(src, dst, sems, slot, dev):
    pltpu.make_async_remote_copy(
        src, dst, sems.at[slot], sems.at[slot + 1], device_id=dev, device_id_type=MESH
    ).start()


def take(ref, sem):
    pltpu.make_async_copy(ref, ref, sem).wait()


def rim_pieces(tile, border, rim, lines, strip):
    pixels = tile.shape[0]
    out = [
        (tile.at[pl.ds(pixels - lines, lines)], rim.at[pl.ds(0, lines)]),
        (tile.at[pl.ds(0, lines)], rim.at[pl.ds(lines, lines)]),
    ]
    at, to = 0, 2 * lines
    for size in (strip, strip, CORNER, CORNER, CORNER, CORNER):
        out.append((border.at[pl.ds(at, size)], rim.at[pl.ds(to, size)]))
        at, to = at + size, to + size
    return tuple(out)


def start_rim(place, pieces, sems):
    for (dr, dc), (src, dst), k in zip(STEPS, pieces, range(8)):
        @pl.when(place.inside(dr, dc))
        def _():
            send(src, dst, sems, 2 * k, place.rim_dev(dr, dc))


def finish_rim(place, pieces, sems):
    for (dr, dc), (_, dst), k in zip(STEPS, pieces, range(8)):
        @pl.when(place.inside(-dr, -dc))
        def _():
            take(dst, sems.at[2 * k + 1])

        @pl.when(jnp.logical_not(place.inside(-dr, -dc)))
        def _():
            dst[...] = jnp.zeros(dst.shape, BF16)


def drain_rim(place, pieces, sems):
    for (dr, dc), (_, dst), k in zip(STEPS, pieces, range(8)):
        @pl.when(place.inside(dr, dc))
        def _():
            take(dst, sems.at[2 * k])


def lines_of(row):
    return jnp.concatenate([row[:, k * 128 : (k + 1) * 128] for k in range(row.shape[1] // 128)], 0)


def row_of(lines):
    return jnp.concatenate([lines[k : k + 1] for k in range(lines.shape[0])], 1)


def merge_moments(buf, count, each):
    half = buf.shape[1] // 2
    means = buf[:, :half]
    mean = jnp.sum(means, axis=0) * (1.0 / count)
    gap = means - mean[None]
    spread = jnp.sum(buf[:, half:], axis=0) + each * jnp.sum(gap * gap, axis=0)
    return jnp.concatenate([mean, spread], axis=0)


def step_kernel(
    rows, cols, radius,
    feat_hbm, cot_hbm, tap_hbm, fin_hbm, frim_hbm, ftap_hbm, fout_hbm, gtap_hbm,
    down_hbm, phase_hbm, border_hbm, win_hbm, wout_hbm, gain, offset, b_in, b_out, scale, b_down,
    coarse_ref, grad_in_ref, grad_tap_ref,
    feat, cot, tap_raw, fin, frim, ftap, fout, gtap, down, phase, choose, win, wout,
    cot32, spread, cot_in, coarse_in, taps, tap_spec, mixed, spec, own, conv, grad, xgrad, act,
    border, rim, planes,
    near_buf, far_buf, near_sum, far_sum, mine, mid, sums, sums_mid,
    tap_part, tap_near, tap_share, tap_far, tap_all,
    in_sems, rim_sems, sems,
):
    place = Place(rows, cols)
    sources = (
        (cot_hbm, cot), (tap_hbm, tap_raw), (ftap_hbm, ftap), (feat_hbm, feat), (fin_hbm, fin),
        (frim_hbm, frim), (fout_hbm, fout), (down_hbm, down), (phase_hbm, phase),
        (win_hbm, win), (wout_hbm, wout), (gtap_hbm, gtap), (border_hbm, choose),
    )
    loads = [
        pltpu.make_async_copy(src, dst, in_sems.at[k]) for k, (src, dst) in enumerate(sources)
    ]
    for k in (3, 12, 0, 1, 2, 4, 5, 6, 7, 8, 10, 9, 11):
        loads[k].start()
    place.greet()

    outs, lines, width = cot.shape
    pixels, channels = conv.shape
    side = pixels // (2 * lines)
    parts_n = pixels // CHUNK
    area = (2 * lines + 2 * radius) * (side + 2 * radius)
    everything = float(pixels * rows * cols)
    zero = jnp.zeros((1, channels), F32)
    strip = 2 * lines * radius
    pieces = rim_pieces(feat, border, rim, radius * side, strip)

    def cut_border():
        @pl.loop(0, border.shape[0] // strip)
        def _(m):
            border[rows_of(m, strip)] = fdot(choose[rows_of(m, strip)], feat[...]).astype(BF16)

    loads[3].wait()
    loads[12].wait()
    cut_border()

    loads[0].wait()
    for tg in range(width // 128):
        cot32[tg] = cot[:, :, tg * 128 : (tg + 1) * 128].astype(F32).reshape(outs * lines, 128)
        for pg in range(lines // 8):
            parts = swap_blocks([
                cot32[tg, pl.ds(pg * 8 + k, outs, stride=lines), :] for k in range(8)
            ])
            for k in range(8):
                spread[tg * 8 + k, :, pg * 128 : (pg + 1) * 128] = parts[k].astype(BF16)
    place.met()
    start_rim(place, pieces, rim_sems)

    loads[1].wait()
    loads[2].wait()
    taps[...] = jnp.zeros(taps.shape, BF16)
    for i in range(2 * radius + 1):
        taps[i * TAP_LINE : i * TAP_LINE + 2 * radius + 1] = tap_raw[i]

    @pl.loop(0, 2 * HALF // CHUNK)
    def _(m):
        tap_spec[rows_of(m)] = fdot(ftap[rows_of(m)], taps[...])

    loads[4].wait()

    @pl.loop(0, 2 * HALF // CHUNK)
    def _(m):
        spec[rows_of(m)] = fdot(fin[rows_of(m)], feat[...])

    finish_rim(place, pieces, rim_sems)
    for k in range(1, cols):
        peer, dev = place.col_dev(k)
        send(spread.at[peer], cot_in.at[place.c], sems, 0, dev)
    cot_in[place.c] = spread[place.c]
    loads[5].wait()

    @pl.loop(0, HALF // CHUNK)
    def _(m):
        re, im = rows_of(m), rows_of(m + HALF // CHUNK)
        fr = spec[re] + fdot(frim[re], rim[...])
        fi = spec[im] + fdot(frim[im], rim[...])
        spec[re], spec[im] = fr, fi
        kr, ki = tap_spec[re], tap_spec[im]
        mixed[re] = (fr * kr + fi * ki).astype(BF16)
        mixed[im] = (fi * kr - fr * ki).astype(BF16)

    loads[6].wait()

    def invert(m, total):
        block = fdot(fout[rows_of(m)], mixed[...]) * (1.0 / area)
        conv[rows_of(m)] = block
        return total + jnp.sum(block, axis=0, keepdims=True)

    local = lax.fori_loop(0, parts_n, invert, zero) * (1.0 / pixels)

    def scatter(m, total):
        gap = conv[rows_of(m)] - local
        return total + jnp.sum(gap * gap, axis=0, keepdims=True)

    around = lax.fori_loop(0, parts_n, scatter, zero)
    mine[...] = jnp.concatenate([lines_of(local), lines_of(around)], axis=0)
    for k in range(1, place.nears):
        send(mine, near_buf.at[place.near], sems, 2, place.near_dev(k)[1])
    near_buf[place.near] = mine[...]

    take(cot_in.at[pl.ds(0, cols - 1)], sems.at[1])
    loads[7].wait()
    loads[8].wait()
    tall = cot_in[...].reshape(cols * outs, lines * lines).astype(F32).T.astype(BF16)
    for ab in range(4):
        planes[ab] = ndot(tall, down[ab]).astype(BF16)
    take(near_buf.at[pl.ds(0, place.nears - 1)], sems.at[3])
    mid[...] = merge_moments(near_buf, place.nears, float(pixels))
    for k in range(1, place.fars):
        send(mid, far_buf.at[place.far], sems, 4, place.far_dev(k)[1])
    far_buf[place.far] = mid[...]
    for k in range(parts_n):
        block = jnp.concatenate([planes[ab, k * 64 : (k + 1) * 64] for ab in range(4)], axis=0)
        grad[k * CHUNK : (k + 1) * CHUNK] = lax.dot_general(
            phase[...], block, (((0,), (0,)), ((), ())), preferred_element_type=F32
        ).astype(BF16)
    take(far_buf.at[pl.ds(0, place.fars - 1)], sems.at[5])
    moments = merge_moments(far_buf, place.fars, float(pixels * place.nears))
    take(cot_in.at[pl.ds(0, cols - 1)], sems.at[0])
    drain_rim(place, pieces, rim_sems)

    half = moments.shape[0] // 2
    mean = row_of(moments[:half])
    inverse = lax.rsqrt(row_of(moments[half:]) * (1.0 / everything) + 1e-05)
    loads[9].wait()
    loads[10].wait()
    hidden = win.shape[1]
    step = 512

    def mlp(m, totals):
        at = rows_of(m)
        xhat = (conv[at] - mean) * inverse
        normed = (xhat * gain[...] + offset[...]).astype(BF16)
        scaled = (scale[...] * grad[at].astype(F32)).astype(BF16)
        back = jnp.zeros((CHUNK, channels), F32)
        cuts = [slice(j, j + step) for j in range(0, hidden, step)]

        def enter(cut):
            return fdot(normed, win[:, cut]) + b_in[:, cut], ndot(scaled, wout[cut])

        ready = enter(cuts[0])
        for cut, after in zip(cuts, cuts[1:] + [None]):
            v, act_grad = ready
            if after is not None:
                ready = enter(after)
            square = v * v
            gate = 0.5 * jnp.tanh(v * (GELU_A + (GELU_A * GELU_B) * square)) + 0.5
            act[at, cut] = (v * gate).astype(BF16)
            bend = v * (2.0 * GELU_A + (6.0 * GELU_A * GELU_B) * square)
            slope = gate * ((1.0 - gate) * bend + 1.0)
            back = back + ndot((act_grad * slope).astype(BF16), win[:, cut])
        back = back * gain[...]
        xgrad[at] = back
        return (
            totals[0] + jnp.sum(back, axis=0, keepdims=True),
            totals[1] + jnp.sum(back * xhat, axis=0, keepdims=True),
        )

    total, product = lax.fori_loop(0, parts_n, mlp, (zero, zero))
    sums[...] = jnp.concatenate([lines_of(total), lines_of(product)], axis=0)
    for k in range(1, place.nears):
        send(sums, near_sum.at[place.near], sems, 6, place.near_dev(k)[1])
    near_sum[place.near] = sums[...]

    for k in range(parts_n):
        at = slice(k * CHUNK, (k + 1) * CHUNK)
        branch = fdot(act[at], wout[...]) + b_out[...]
        summed = (feat[at].astype(F32) + scale[...] * branch).astype(BF16)
        split = fdot(phase[...], summed).astype(BF16)
        for ab in range(4):
            planes[ab, k * 64 : (k + 1) * 64] = split[ab * 64 : (ab + 1) * 64]
    take(near_sum.at[pl.ds(0, place.nears - 1)], sems.at[7])
    sums_mid[...] = jnp.sum(near_sum[...], axis=0)
    for k in range(1, place.fars):
        send(sums_mid, far_sum.at[place.far], sems, 8, place.far_dev(k)[1])
    far_sum[place.far] = sums_mid[...]
    flat = b_down[...]
    for ab in range(4):
        flat = flat + fdot(planes[ab], down[ab])
    spread[...] = flat.T.astype(BF16).reshape(cols, outs, lines * lines)
    take(far_sum.at[pl.ds(0, place.fars - 1)], sems.at[9])
    both = jnp.sum(far_sum[...], axis=0) * (1.0 / everything)
    level, slant = row_of(both[:half]), row_of(both[half:])

    for k in range(parts_n):
        at = slice(k * CHUNK, (k + 1) * CHUNK)
        xhat = (conv[at] - mean) * inverse
        feat[at] = (inverse * (xgrad[at] - level - xhat * slant)).astype(BF16)
    cut_border()
    start_rim(place, pieces, rim_sems)

    @pl.loop(0, HALF // CHUNK)
    def _(m):
        re, im = rows_of(m), rows_of(m + HALF // CHUNK)
        gr, gi = fdot(fin[re], feat[...]), fdot(fin[im], feat[...])
        own[re], own[im] = gr, gi
        fr, fi = spec[re], spec[im]
        mixed[re] = (fr * gr + fi * gi).astype(BF16)
        mixed[im] = (fi * gr - fr * gi).astype(BF16)

    loads[11].wait()
    norm = 1.0 / (area * float(np.sqrt(everything)))
    tap_part[...] = (fdot(gtap[...], mixed[...]) * norm).reshape(tap_part.shape).astype(BF16)

    def tap_block(index):
        start = pl.multiple_of((index % NEAR_X) * 128, 128)
        return tap_part.at[pl.ds((index // NEAR_X) * TAP_TILES, TAP_TILES), :, pl.ds(start, 128)]

    for k in range(1, place.nears):
        peer, dev = place.near_dev(k)
        send(tap_block(peer), tap_near.at[place.near], sems, 12, dev)
    tap_near[place.near] = tap_block(place.near)[...]

    finish_rim(place, pieces, rim_sems)
    for k in range(1, cols):
        peer, dev = place.col_dev(k)
        send(spread.at[peer], coarse_in.at[place.c], sems, 10, dev)
    coarse_in[place.c] = spread[place.c]

    @pl.loop(0, HALF // CHUNK)
    def _(m):
        re, im = rows_of(m), rows_of(m + HALF // CHUNK)
        gr = own[re] + fdot(frim[re], rim[...])
        gi = own[im] + fdot(frim[im], rim[...])
        kr, ki = tap_spec[re], tap_spec[im]
        mixed[re] = (gr * kr - gi * ki).astype(BF16)
        mixed[im] = (gr * ki + gi * kr).astype(BF16)

    take(tap_near.at[pl.ds(0, place.nears - 1)], sems.at[13])
    tap_share[...] = jnp.sum(tap_near[...].astype(F32), axis=0).astype(BF16)
    for k in range(1, place.fars):
        send(tap_share, tap_far.at[place.far], sems, 14, place.far_dev(k)[1])
    tap_far[place.far] = tap_share[...]

    @pl.loop(0, parts_n)
    def _(m):
        at = rows_of(m)
        block = fdot(fout[at], mixed[...]) * (1.0 / area)
        grad_in_ref[at] = (grad[at].astype(F32) + block).astype(BF16)

    take(tap_far.at[pl.ds(0, place.fars - 1)], sems.at[15])
    tap_all[place.near] = jnp.sum(tap_far[...].astype(F32), axis=0).astype(BF16)
    for k in range(1, place.nears):
        send(tap_all.at[place.near], tap_all.at[place.near], sems, 16, place.near_dev(k)[1])

    take(coarse_in.at[pl.ds(0, cols - 1)], sems.at[11])
    for tg in range(width // 128):
        for pg in range(lines // 8):
            parts = swap_blocks([
                coarse_in[tg * 8 + k, :, pg * 128 : (pg + 1) * 128].astype(F32) for k in range(8)
            ])
            for k in range(8):
                cot32[tg, pl.ds(pg * 8 + k, outs, stride=lines), :] = parts[k]
        coarse_ref[:, :, tg * 128 : (tg + 1) * 128] = (
            cot32[tg].reshape(outs, lines, 128).astype(BF16)
        )
    take(tap_near.at[pl.ds(0, place.nears - 1)], sems.at[17])
    for i in range(2 * radius + 1):
        for b in range(NEAR_X):
            line = tap_all[(i // TAP_TILES) * NEAR_X + b, i % TAP_TILES].astype(F32)
            grad_tap_ref[i, :, b * 128 : (b + 1) * 128] = line[: 2 * radius + 1]
    drain_rim(place, pieces, rim_sems)
    take(near_buf.at[pl.ds(0, place.nears - 1)], sems.at[2])
    take(far_buf.at[pl.ds(0, place.fars - 1)], sems.at[4])
    take(near_sum.at[pl.ds(0, place.nears - 1)], sems.at[6])
    take(far_sum.at[pl.ds(0, place.fars - 1)], sems.at[8])
    take(coarse_in.at[pl.ds(0, cols - 1)], sems.at[10])
    take(tap_near.at[pl.ds(0, place.nears - 1)], sems.at[12])
    take(tap_far.at[pl.ds(0, place.fars - 1)], sems.at[14])
    take(tap_near.at[pl.ds(0, place.nears - 1)], sems.at[16])


def hand_over(a_in, b_in, c_in, a_out, b_out, c_out, a, b, c, sems):
    enter = [
        pltpu.make_async_copy(src, dst, sems.at[k])
        for k, (src, dst) in enumerate(((a_in, a), (b_in, b), (c_in, c)))
    ]
    leave = [
        pltpu.make_async_copy(src, dst, sems.at[3 + k])
        for k, (src, dst) in enumerate(((a, a_out), (b, b_out), (c, c_out)))
    ]
    for copy in enter:
        copy.start()
    for arrive, go in zip(enter, leave):
        arrive.wait()
        go.start()
    for copy in leave:
        copy.wait()


def per_device(
    features, dw_kernel, batchnorm_gain, batchnorm_offset, w_in, b_in, w_out, b_out,
    layer_scale, w_down, b_down, cotangent,
):
    rows, cols = lax.axis_size("rows"), lax.axis_size("cols")
    tile_h, tile_w, channels = features.shape
    radius = (dw_kernel.shape[0] - 1) // 2
    pixels = tile_h * tile_w
    tables = [jnp.asarray(t) for t in dft_tables(tile_h, tile_w, radius)]
    outs, lines, width = cotangent.shape
    hidden = w_in.shape[1]
    far = (
        features.reshape(pixels, channels),
        cotangent,
        dw_kernel,
        *tables,
        w_down.reshape(4, channels, w_down.shape[-1]),
        jnp.asarray(phase_table(tile_w)),
        jnp.asarray(border_table(tile_h, tile_w, radius)),
        w_in,
        w_out,
    )
    near = tuple(
        v.reshape(1, -1)
        for v in (batchnorm_gain, batchnorm_offset, b_in, b_out, layer_scale, b_down)
    )
    stats = (2 * channels // 128, 128)
    nears, fars = rows * NEAR_X, cols // NEAR_X
    vm = pltpu.VMEM
    scratch = [vm(a.shape, BF16) for a in far]
    scratch += [
        vm((width // 128, outs * lines, 128), F32),
        vm((cols, outs, lines * lines), BF16),
        vm((cols, outs, lines * lines), BF16),
        vm((cols, outs, lines * lines), BF16),
        vm((CHUNK, channels), BF16),
        vm((2 * HALF, channels), F32),
        vm((2 * HALF, channels), BF16),
        vm((2 * HALF, channels), F32),
        vm((2 * HALF, channels), F32),
        vm((pixels, channels), F32),
        vm((pixels, channels), BF16),
        vm((pixels, channels), F32),
        vm((pixels, hidden), BF16),
        vm((far[-3].shape[0], channels), BF16),
        vm((tables[1].shape[1], channels), BF16),
        vm((4, pixels // 4, channels), BF16),
        vm((nears,) + stats, F32),
        vm((fars,) + stats, F32),
        vm((nears,) + stats, F32),
        vm((fars,) + stats, F32),
        vm(stats, F32),
        vm(stats, F32),
        vm(stats, F32),
        vm(stats, F32),
        vm((TAP_ROWS // TAP_LINE, TAP_LINE, channels), BF16),
        vm((nears, TAP_TILES, TAP_LINE, 128), BF16),
        vm((TAP_TILES, TAP_LINE, 128), BF16),
        vm((fars, TAP_TILES, TAP_LINE, 128), BF16),
        vm((nears, TAP_TILES, TAP_LINE, 128), BF16),
        pltpu.SemaphoreType.DMA((13,)),
        pltpu.SemaphoreType.DMA((16,)),
        pltpu.SemaphoreType.DMA((18,)),
    ]
    results = pl.pallas_call(
        functools.partial(step_kernel, rows, cols, radius),
        out_shape=(
            jax.ShapeDtypeStruct(cotangent.shape, BF16),
            jax.ShapeDtypeStruct((pixels, channels), BF16),
            jax.ShapeDtypeStruct(dw_kernel.shape, F32),
        ),
        in_specs=[pl.BlockSpec(memory_space=pl.ANY)] * len(far)
        + [pl.BlockSpec(memory_space=pltpu.VMEM)] * len(near),
        out_specs=[pl.BlockSpec(memory_space=pltpu.VMEM)] * 3,
        scratch_shapes=scratch,
        compiler_params=pltpu.CompilerParams(
            collective_id=1, has_side_effects=True, vmem_limit_bytes=67043328
        ),
        name="step",
    )(*far, *near)
    coarse, grad_input, grad_kernel = pl.pallas_call(
        hand_over,
        out_shape=tuple(jax.ShapeDtypeStruct(a.shape, a.dtype) for a in results),
        in_specs=[pl.BlockSpec(memory_space=pl.ANY)] * 3,
        out_specs=[pl.BlockSpec(memory_space=pl.ANY)] * 3,
        scratch_shapes=[vm(a.shape, a.dtype) for a in results] + [pltpu.SemaphoreType.DMA((6,))],
        name="hand_over",
    )(*results)
    return coarse, grad_input.reshape(features.shape), grad_kernel


def solution(mesh):
    in_specs = (
        P("rows", "cols", None),
        P(),
        P(),
        P(),
        P(),
        P(),
        P(),
        P(),
        P(),
        P(),
        P(),
        P("cols", "rows", None),
    )
    out_specs = (P("cols", "rows", None), P("rows", "cols", None), P())
    return jax.shard_map(
        per_device, mesh=mesh, in_specs=in_specs, out_specs=out_specs, check_vma=False
    )
```
